32 devices in a mesh: groups: 2 (over y), ctx: 16 (over z, x, core).
Axes of the slice: x: 2, y: 2, z: 4, core: 2. Of those that a mesh axis runs over, the one named last changes fastest.
Arguments:
- signal: bfloat16 [4096, 4096], P(None, ('groups', 'ctx')), parts along dimension 1, may hold values from -6 to 6
- input_gate: bfloat16 [4096, 4096], P(None, ('groups', 'ctx')), parts along dimension 1, may hold values from -6 to 6
- output_gate: bfloat16 [4096, 4096], P(None, ('groups', 'ctx')), parts along dimension 1, may hold values from -6 to 6
- short_taps: bfloat16 [3, 4096, 7], replicated, may hold values from -2 to 2
- long_filter: bfloat16 [4096, 2048], P('ctx'), may hold values from -0.125 to 0.125
- bypass_gain: float32 [4096], P('ctx'), may hold values from 0.5 to 1.5
Outputs:
- mixed: bfloat16 [4096, 4096], P(None, ('groups', 'ctx')), parts along dimension 1
The draws below stay inside these ranges and needn't reach their ends.
There are 2 independent parts, one for each index of `groups`. The reference program is written for one: setup_inputs(seed, part) draws one part's arguments, and reference() takes and returns one part's arrays. A program takes and returns all parts, laid end to end along the dimension named above; an argument that names none is the same for every part. Nothing has to cross between parts.
All inputs are finite; a program needn't handle non-finite values.
Results may differ from the reference program's by a relative error of at most 0.0065.
Values may be sent and summed in bfloat16 or wider, within the bound.
No kernel may reach another device: no remote copies, remote signals or barrier semaphores. Data moves between devices by JAX's collectives and lax.ppermute only.
A program may use at most 128 MiB of HBM per device.

```python
import math
import jax
import jax.numpy as jnp
from jax import lax

D = 4096
STAPS = 7
TOKENS = 2048


def steps_of(stream_key, extent, shards, least, top_value):
    gain, own = 1.0, jax.random.fold_in(stream_key, 6)
    for position, shards_of in shards:
        heights = jnp.exp(jax.random.uniform(jax.random.fold_in(own, position), (shards_of,), jnp.float32, least / len(shards), top_value / len(shards)))
        gain = gain * jnp.repeat(heights, extent[position] // shards_of).reshape([-1 if axis == position else 1 for axis in range(len(extent))])
    return gain


def bell_draw(stream_key, shape, width, bound, pieces=(), held_as=jnp.bfloat16):
    drawn = width * jax.random.normal(stream_key, shape, jnp.float32)
    if pieces:
        drawn = drawn * steps_of(stream_key, shape, pieces, -0.22, 0.18)
    return jnp.clip(drawn, -bound, bound).astype(held_as)


def setup_inputs(seed: int = 0, part: int = 0) -> dict:
    streams_of = jax.random.split(jax.random.key(seed), 7)
    part_keys = jax.random.split(jax.random.fold_in(streams_of[6], part), 7)
    return {
        "signal": bell_draw(part_keys[0], (D, TOKENS), 1.0, 6.0, ((1, 16),)),
        "input_gate": bell_draw(part_keys[1], (D, TOKENS), 1.0, 6.0, ((1, 16),)),
        "output_gate": bell_draw(part_keys[2], (D, TOKENS), 1.0, 6.0, ((1, 16),)),
        "short_taps": bell_draw(streams_of[3], (3, D, STAPS), STAPS ** -0.5, 2.0),
        "long_filter": bell_draw(streams_of[4], (D, TOKENS), TOKENS ** -0.5, 0.125, ((0, 16),)),
        "bypass_gain": jnp.clip(0.5 + 1.0 * jax.random.uniform(streams_of[5], (D,), jnp.float32) ** steps_of(streams_of[5], (D,), ((0, 16),), -0.2, 0.2), 0.5, 1.5),
    }


def short_conv(values, taps):
    tap_count = taps.shape[1]
    length = values.shape[1]
    padded = jnp.concatenate([jnp.zeros((values.shape[0], tap_count - 1), values.dtype), values], axis=1)
    total = jnp.zeros_like(values)
    for k in range(tap_count):
        total = total + taps[:, k:k + 1] * padded[:, tap_count - 1 - k:tap_count - 1 - k + length]
    return total


def long_conv(gated_f, kernel, bypass):
    channels, length = gated_f.shape
    block = math.gcd(channels, 256)

    def per_block(member):
        piece_sig, piece_ker, piece_gain = member
        spectrum = jnp.fft.rfft(piece_sig, n=2 * length, axis=-1) * jnp.fft.rfft(piece_ker, n=2 * length, axis=-1)
        back = jnp.fft.irfft(spectrum, n=2 * length, axis=-1)[:, :length]
        return back + piece_gain[:, None] * piece_sig

    result = lax.map(per_block, (gated_f.reshape(channels // block, block, length),
                                 kernel.reshape(channels // block, block, length),
                                 bypass.reshape(channels // block, block)))
    return result.reshape(channels, length)


def reference(signal, input_gate, output_gate, short_taps, long_filter, bypass_gain):
    taps = short_taps.astype(jnp.float32)
    feat_value = short_conv(signal.astype(jnp.float32), taps[0])
    feat_key = short_conv(input_gate.astype(jnp.float32), taps[1])
    feat_query = short_conv(output_gate.astype(jnp.float32), taps[2])
    gated_mid = (feat_key * feat_value).astype(jnp.bfloat16)
    gated_f = lax.optimization_barrier(gated_mid).astype(jnp.float32)
    longconv = long_conv(gated_f, long_filter.astype(jnp.float32), bypass_gain)
    long_rounded = lax.optimization_barrier(longconv.astype(jnp.bfloat16))
    return (feat_query * long_rounded.astype(jnp.float32)).astype(jnp.bfloat16)
```

```python
import functools
import math

import jax
import jax.numpy as jnp
import numpy as np
from jax import lax
from jax.experimental import pallas as pl
from jax.experimental.pallas import tpu as pltpu
from jax.sharding import PartitionSpec as P

F32, BF16 = jnp.float32, jnp.bfloat16
VMEM_LIMIT = 40 << 20
LANES = 128


def shifted(shard, axis, by):
    count = lax.axis_size(axis)
    pairs = [(i, i + by) for i in range(count) if 0 <= i + by < count]
    return lax.ppermute(shard, axis, pairs)


def short_conv(values, taps, rim):
    tap_count = taps.shape[1]
    length = values.shape[1]
    padded = jnp.concatenate([rim, values], axis=1)
    total = jnp.zeros_like(values)
    for k in range(tap_count):
        total = (
            total + taps[:, k : k + 1] * padded[:, tap_count - 1 - k : tap_count - 1 - k + length]
        )
    return total


def dft_tables(height, breadth, period):
    rindex = lax.broadcasted_iota(jnp.int32, (height, breadth), 0)
    cindex = lax.broadcasted_iota(jnp.int32, (height, breadth), 1)
    phase_angle = (rindex * cindex % period).astype(F32) * (2.0 * math.pi / period)
    return (jnp.cos(phase_angle), jnp.sin(phase_angle))


def split_table(table):
    upper = table.astype(BF16)
    lower = (table - upper.astype(F32)).astype(BF16)
    return (upper, lower)


def precise(pattern, left_op, right_op):
    return jnp.einsum(pattern, left_op, right_op, precision=lax.Precision.HIGHEST)


def narrow(pattern, parts, right_op):
    first = jnp.einsum(pattern, parts[0], right_op, preferred_element_type=F32)
    return first + jnp.einsum(pattern, parts[1], right_op, preferred_element_type=F32)


def make_tables(length):
    breadth = 128
    height = 2 * length // breadth
    row_tables = dft_tables(height, height // 2, height)
    twist_tables = dft_tables(height, breadth, 2 * length)
    col_tables = dft_tables(breadth, breadth, breadth)
    row_split = (split_table(row_tables[0]), split_table(row_tables[1]))
    return (row_tables, twist_tables, col_tables, row_split)


def forward_dft(values, tables):
    row_tables, twist_tables, col_tables, row_split = tables
    chan_count, length = values.shape
    folded = values.reshape(chan_count, length // 128, 128)
    first_re = narrow("kp,cpq->ckq", row_split[0], folded)
    first_im = -narrow("kp,cpq->ckq", row_split[1], folded)
    turned_re = first_re * twist_tables[0] + first_im * twist_tables[1]
    turned_im = first_im * twist_tables[0] - first_re * twist_tables[1]
    spec_re = precise("ckq,qm->ckm", turned_re, col_tables[0]) + precise(
        "ckq,qm->ckm", turned_im, col_tables[1]
    )
    spec_im = precise("ckq,qm->ckm", turned_im, col_tables[0]) - precise(
        "ckq,qm->ckm", turned_re, col_tables[1]
    )
    return (spec_re, spec_im)


def inverse_dft(spec_re, spec_im, tables, length):
    row_tables, twist_tables, col_tables, row_split = tables
    chan_count = spec_re.shape[0]
    back_re = precise("ckm,mq->ckq", spec_re, col_tables[0]) - precise(
        "ckm,mq->ckq", spec_im, col_tables[1]
    )
    back_im = precise("ckm,mq->ckq", spec_re, col_tables[1]) + precise(
        "ckm,mq->ckq", spec_im, col_tables[0]
    )
    twist_re = back_re * twist_tables[0] - back_im * twist_tables[1]
    twist_im = back_re * twist_tables[1] + back_im * twist_tables[0]
    folded = precise("kp,ckq->cpq", row_tables[0], twist_re) - precise(
        "kp,ckq->cpq", row_tables[1], twist_im
    )
    return (folded / (2.0 * length)).reshape(chan_count, length)


def long_mix(gated_narrow, kernel, bypass):
    length = gated_narrow.shape[1]
    tables = make_tables(length)
    kern_re, kern_im = forward_dft(kernel, tables)
    sig_re, sig_im = forward_dft(gated_narrow, tables)
    prod_re = sig_re * kern_re - sig_im * kern_im
    prod_im = sig_re * kern_im + sig_im * kern_re
    return inverse_dft(prod_re, prod_im, tables, length) + bypass[:, None] * gated_narrow.astype(
        F32
    )


def general_path(signal, input_gate, output_gate, short_taps, long_filter, bypass_gain):
    channels, local_tokens = signal.shape
    rim_len = short_taps.shape[2] - 1
    taps = short_taps.astype(F32)
    feats = []
    for i, stream in enumerate((signal, input_gate, output_gate)):
        rim = shifted(stream[:, local_tokens - rim_len :], "ctx", 1)
        feats.append(short_conv(stream.astype(F32), taps[i], rim.astype(F32)))
    gated = (feats[1] * feats[0]).astype(BF16)
    gated = lax.all_to_all(gated, "ctx", split_axis=0, concat_axis=1, tiled=True)
    longconv = long_mix(gated, long_filter, bypass_gain).astype(BF16)
    returned = lax.all_to_all(longconv, "ctx", split_axis=1, concat_axis=0, tiled=True)
    return (feats[2] * returned.astype(F32)).astype(BF16)


def add(a, b):
    return b if a is None else a if b is None else a + b


def sub(a, b):
    return a if b is None else -b if a is None else a - b


def turn(value, k, n):
    re, im = value
    k %= n
    if k == 0:
        return value
    if 4 * k == n:
        return (None if im is None else -im, re)
    if 4 * k == 3 * n:
        return (im, None if re is None else -re)
    c, s = math.cos(2 * math.pi * k / n), math.sin(2 * math.pi * k / n)
    if im is None:
        return (re * c, re * s)
    if re is None:
        return (im * -s, im * c)
    return (re * c - im * s, re * s + im * c)


def rfft(xs):
    n = len(xs)
    if n == 1:
        return [(xs[0], None)]
    half = n // 2
    even, odd = rfft(xs[0::2]), rfft(xs[1::2])
    out = [None] * (half + 1)
    for k in range(half // 2 + 1):
        e, t = even[k], turn(odd[k], -k, n)
        out[k] = (add(e[0], t[0]), add(e[1], t[1]))
        if half - k != k:
            out[half - k] = (sub(e[0], t[0]), sub(t[1], e[1]))
    return out


def irfft_first_half(zs):
    half = len(zs) - 1
    n = 2 * half
    if n == 2:
        return [add(zs[0][0], zs[1][0])]
    even, odd = [], []
    for k in range(half // 2 + 1):
        a, b = zs[k], zs[half - k]
        if k == half - k:
            even.append((a[0] * 2.0, None))
            odd.append((a[1] * -2.0, None))
            continue
        even.append((add(a[0], b[0]), sub(a[1], b[1])))
        odd.append(turn((sub(a[0], b[0]), add(a[1], b[1])), k, n))
    first, second = irfft_first_half(even), irfft_first_half(odd)
    return [v for pair in zip(first, second) for v in pair]


def hi_lo(value):
    upper = value.astype(BF16)
    return upper, (value - upper.astype(F32)).astype(BF16)


def np_hi_lo(table):
    table = table.astype(np.float32)
    upper = table.astype(jnp.bfloat16)
    return upper, (table - upper.astype(np.float32)).astype(jnp.bfloat16)


def transform_tables(blocks, inner):
    period = 2 * blocks * inner
    index = np.arange(inner)
    angle = 2 * np.pi * (np.outer(index, index) % inner) / inner
    c, s = np.cos(angle), np.sin(angle)
    wh, wl = np_hi_lo(np.block([[c, s], [-s, c]]))
    vh, vl = np_hi_lo(np.block([[c, -s], [s, c]]) / period)
    forward = np.concatenate([wh, wh, wl], axis=1)
    backward = np.concatenate([vh, vh, vl], axis=1)
    freqs = np.arange(blocks + 1)
    turns = 2 * np.pi * np.outer(index, freqs) / period
    table = np.zeros((inner, 2 * LANES), np.float32)
    table[:, : blocks + 1] = np.cos(turns)
    table[:, LANES : LANES + blocks + 1] = np.sin(turns)
    return jnp.asarray(forward), jnp.asarray(backward), jnp.asarray(table)


ROWS = 16


def over_tiles(rows, lanes, body):
    row_tiles = rows // ROWS

    def step(t, carry):
        body(
            pl.multiple_of(t % row_tiles * ROWS, ROWS),
            pl.multiple_of(t // row_tiles * LANES, LANES),
        )
        return carry

    lax.fori_loop(0, row_tiles * (lanes // LANES), step, 0)


def outer_forward(src_ref, turn_ref, hi_ref, lo_ref):
    blocks, inner, chans = src_ref.shape

    def tile(row, lane):
        xs = [src_ref[b, pl.ds(row, ROWS), pl.ds(lane, LANES)].astype(F32) for b in range(blocks)]
        for k, (re, im) in enumerate(rfft(xs + [None] * blocks)):
            if k:
                c = turn_ref[pl.ds(row, ROWS), k : k + 1]
                s = turn_ref[pl.ds(row, ROWS), LANES + k : LANES + k + 1]
                if im is None:
                    re, im = re * c, -(re * s)
                else:
                    re, im = re * c + im * s, im * c - re * s
            if im is None:
                im = jnp.zeros_like(re)
            for part, base in ((re, 0), (im, inner)):
                upper, lower = hi_lo(part)
                hi_ref[k, pl.ds(base + row, ROWS), pl.ds(lane, LANES)] = upper
                lo_ref[k, pl.ds(base + row, ROWS), pl.ds(lane, LANES)] = lower

    over_tiles(inner, chans, tile)


def inner_product(table_ref, upper, lower):
    stacked = jnp.concatenate([upper, lower, upper], axis=0)
    return jnp.dot(table_ref[...], stacked, preferred_element_type=F32)


def spectrum_kernel(filt_ref, turn_ref, fwd_ref, spec_ref, hi_ref, lo_ref):
    outer_forward(filt_ref, turn_ref, hi_ref, lo_ref)

    def step(k, carry):
        spec_ref[k] = inner_product(fwd_ref, hi_ref[k], lo_ref[k])
        return carry

    lax.fori_loop(0, spec_ref.shape[0], step, 0)


def conv_kernel(
    gated_ref, spec_ref, gain_ref, turn_ref, fwd_ref, bwd_ref, out_ref, hi_ref, lo_ref, back_ref
):
    blocks, inner, chans = gated_ref.shape
    outer_forward(gated_ref, turn_ref, hi_ref, lo_ref)

    def step(k, carry):
        sig = inner_product(fwd_ref, hi_ref[k], lo_ref[k])
        sig_re, sig_im = sig[:inner], sig[inner:]
        ker_re, ker_im = spec_ref[k, :inner], spec_ref[k, inner:]
        prod = jnp.concatenate(
            [sig_re * ker_re - sig_im * ker_im, sig_re * ker_im + sig_im * ker_re], axis=0
        )
        back_ref[k] = inner_product(bwd_ref, *hi_lo(prod))
        return carry

    lax.fori_loop(0, blocks + 1, step, 0)

    def tile(row, lane):
        zs = []
        for k in range(blocks + 1):
            re = back_ref[k, pl.ds(row, ROWS), pl.ds(lane, LANES)]
            if k == 0:
                zs.append((re, None))
                continue
            im = back_ref[k, pl.ds(inner + row, ROWS), pl.ds(lane, LANES)]
            c = turn_ref[pl.ds(row, ROWS), k : k + 1]
            s = turn_ref[pl.ds(row, ROWS), LANES + k : LANES + k + 1]
            if k == blocks:
                zs.append((re * c - im * s, None))
            else:
                zs.append((re * c - im * s, re * s + im * c))
        gain = gain_ref[:, pl.ds(lane, LANES)]
        for b, value in enumerate(irfft_first_half(zs)):
            held = gated_ref[b, pl.ds(row, ROWS), pl.ds(lane, LANES)].astype(F32)
            out_ref[b, pl.ds(row, ROWS), pl.ds(lane, LANES)] = (value + gain * held).astype(BF16)

    over_tiles(inner, chans, tile)


def filter_spectrum(filt, tables):
    forward, _, turns = tables
    blocks, inner, chans = filt.shape
    return pl.pallas_call(
        spectrum_kernel,
        out_shape=jax.ShapeDtypeStruct((blocks + 1, 2 * inner, chans), F32),
        scratch_shapes=[pltpu.VMEM((blocks + 1, 2 * inner, chans), BF16)] * 2,
        compiler_params=pltpu.CompilerParams(vmem_limit_bytes=VMEM_LIMIT),
        cost_estimate=pl.CostEstimate(flops=4 * 10**9, bytes_accessed=8 << 20, transcendentals=0),
        name="filter_spectrum",
    )(filt, turns, forward)


def long_conv(gated, spectrum, gain, tables):
    forward, backward, turns = tables
    blocks, inner, chans = gated.shape
    return pl.pallas_call(
        conv_kernel,
        out_shape=jax.ShapeDtypeStruct(gated.shape, BF16),
        scratch_shapes=[pltpu.VMEM((blocks + 1, 2 * inner, chans), BF16)] * 2
        + [pltpu.VMEM((blocks + 1, 2 * inner, chans), F32)],
        compiler_params=pltpu.CompilerParams(vmem_limit_bytes=VMEM_LIMIT),
        cost_estimate=pl.CostEstimate(flops=8 * 10**9, bytes_accessed=8 << 20, transcendentals=0),
        name="long_conv",
    )(gated, spectrum, gain, turns, forward, backward)


PAD = 8


def short_sum(pad_ref, taps_ref, stream, lane, rows):
    total = None
    for k in range(taps_ref.shape[1]):
        tap = taps_ref[stream, k : k + 1, pl.ds(lane, LANES)]
        term = tap * pad_ref[pl.ds(PAD - k, rows), :]
        total = term if total is None else total + term
    return total


def gate_kernel(sig_ref, key_ref, taps_ref, out_ref, head_ref, pad_ref):
    rows = sig_ref.shape[1]
    pad_ref[:, :PAD] = jnp.zeros((2, PAD, LANES), F32)
    for lane in range(0, sig_ref.shape[0], LANES):
        feats = []
        for i, ref in enumerate((sig_ref, key_ref)):
            turned = ref[pl.ds(lane, LANES), :].astype(F32).T
            pad_ref[i, pl.ds(PAD, rows), :] = turned
            head_ref[i, :, pl.ds(lane, LANES)] = turned[:ROWS]
            feats.append(short_sum(pad_ref.at[i], taps_ref, i, lane, rows))
        out_ref[0, :, pl.ds(lane, LANES)] = (feats[1] * feats[0]).astype(BF16)


def rim_kernel(head_ref, rim_ref, taps_ref, whole_ref, out_ref, pad_ref):
    for block in range(out_ref.shape[0]):
        for part in range(0, out_ref.shape[2], LANES):
            lane = block * out_ref.shape[2] + part
            feats = []
            for i in range(2):
                pad_ref[i, :PAD] = rim_ref[pl.ds(i * PAD, PAD), pl.ds(lane, LANES)].astype(F32)
                pad_ref[i, PAD:] = head_ref[i, :, pl.ds(lane, LANES)]
                feats.append(short_sum(pad_ref.at[i], taps_ref, i, lane, ROWS))
            out_ref[block, :, pl.ds(part, LANES)] = (feats[1] * feats[0]).astype(BF16)


def query_kernel(query_ref, rim_ref, taps_ref, out_ref, pad_ref):
    rows = query_ref.shape[1]
    for lane in range(0, query_ref.shape[0], LANES):
        pad_ref[:PAD] = rim_ref[:, pl.ds(lane, LANES)].astype(F32)
        pad_ref[PAD:] = query_ref[pl.ds(lane, LANES), :].astype(F32).T
        out_ref[0, :, pl.ds(lane, LANES)] = short_sum(pad_ref, taps_ref, 2, lane, rows)


def mix_kernel(conv_ref, query_ref, out_ref):
    for lane in range(0, conv_ref.shape[2], LANES):
        value = conv_ref[0, :, pl.ds(lane, LANES)].astype(F32) * query_ref[0, :, pl.ds(lane, LANES)]
        out_ref[pl.ds(lane, LANES), :] = value.T.astype(BF16)


def fast_path(signal, input_gate, output_gate, short_taps, long_filter, bypass_gain):
    channels, rows = signal.shape
    tap_count = short_taps.shape[2]
    chans, length = long_filter.shape
    blocks = length // rows
    taps = short_taps.astype(F32).transpose(0, 2, 1)
    params = pltpu.CompilerParams(vmem_limit_bytes=VMEM_LIMIT)
    stream_spec = pl.BlockSpec((chans, rows), lambda i: (i, 0))
    taps_spec = pl.BlockSpec((3, tap_count, chans), lambda i: (0, 0, i))
    block_spec = pl.BlockSpec((1, rows, chans), lambda i: (i, 0, 0))

    def last_rows(stream):
        return stream[:, rows - PAD :].T

    rim = shifted(jnp.concatenate([last_rows(signal), last_rows(input_gate)], axis=0), "ctx", 1)
    gated, head = pl.pallas_call(
        gate_kernel,
        grid=(blocks,),
        in_specs=[stream_spec, stream_spec, taps_spec],
        out_specs=[block_spec, pl.BlockSpec((2, ROWS, chans), lambda i: (0, 0, i))],
        out_shape=[
            jax.ShapeDtypeStruct((blocks, rows, chans), BF16),
            jax.ShapeDtypeStruct((2, ROWS, channels), F32),
        ],
        scratch_shapes=[pltpu.VMEM((2, PAD + rows, LANES), F32)],
        compiler_params=params,
        cost_estimate=pl.CostEstimate(flops=10**9, bytes_accessed=8 << 20, transcendentals=0),
        name="gate_main",
    )(signal, input_gate, taps)
    whole = lambda shape: pl.BlockSpec(shape, lambda i: (0,) * len(shape))
    gated = pl.pallas_call(
        rim_kernel,
        grid=(1,),
        in_specs=[
            whole((2, ROWS, channels)),
            whole((2 * PAD, channels)),
            whole((3, tap_count, channels)),
            pl.BlockSpec(memory_space=pl.ANY),
        ],
        out_specs=whole((blocks, ROWS, chans)),
        out_shape=jax.ShapeDtypeStruct((blocks, rows, chans), BF16),
        scratch_shapes=[pltpu.VMEM((2, PAD + ROWS, LANES), F32)],
        input_output_aliases={3: 0},
        compiler_params=params,
        cost_estimate=pl.CostEstimate(flops=10**7, bytes_accessed=1 << 20, transcendentals=0),
        name="gate_rim",
    )(head, rim, taps, gated)
    arrived = lax.all_to_all(gated, "ctx", 0, 0)

    tables = transform_tables(blocks, rows)
    filt = long_filter.reshape(chans, blocks, rows).transpose(1, 2, 0)
    spectrum = filter_spectrum(filt, tables)
    query_rim = shifted(last_rows(output_gate), "ctx", 1)
    query = pl.pallas_call(
        query_kernel,
        grid=(blocks,),
        in_specs=[stream_spec, pl.BlockSpec((PAD, chans), lambda i: (0, i)), taps_spec],
        out_specs=block_spec,
        out_shape=jax.ShapeDtypeStruct((blocks, rows, chans), F32),
        scratch_shapes=[pltpu.VMEM((PAD + rows, LANES), F32)],
        compiler_params=params,
        cost_estimate=pl.CostEstimate(flops=10**9, bytes_accessed=8 << 20, transcendentals=0),
        name="query_feat",
    )(output_gate, query_rim, taps)

    conv = long_conv(arrived, spectrum, bypass_gain.reshape(1, chans), tables)
    returned = lax.all_to_all(conv, "ctx", 0, 0)
    return pl.pallas_call(
        mix_kernel,
        grid=(blocks,),
        in_specs=[block_spec, block_spec],
        out_specs=stream_spec,
        out_shape=jax.ShapeDtypeStruct((channels, rows), BF16),
        compiler_params=params,
        cost_estimate=pl.CostEstimate(flops=10**8, bytes_accessed=4 << 20, transcendentals=0),
        name="mix",
    )(returned, query)


def on_device(signal, input_gate, output_gate, short_taps, long_filter, bypass_gain):
    channels, rows = signal.shape
    chans, length = long_filter.shape
    blocks = length // rows
    fits = (
        rows == LANES
        and chans % LANES == 0
        and chans * blocks == channels
        and blocks * rows == length
        and blocks in (2, 4, 8, 16)
        and short_taps.shape[2] <= PAD
    )
    path = fast_path if fits else general_path
    return path(signal, input_gate, output_gate, short_taps, long_filter, bypass_gain)


def solution(mesh):
    placed = (
        P(None, ("groups", "ctx")),
        P(None, ("groups", "ctx")),
        P(None, ("groups", "ctx")),
        P(),
        P("ctx", None),
        P("ctx"),
    )
    return jax.shard_map(
        on_device, mesh=mesh, in_specs=placed, out_specs=P(None, ("groups", "ctx")), check_vma=False
    )
```

```python
import functools
import math

import jax
import jax.numpy as jnp
import numpy as np
from jax import lax
from jax.experimental import pallas as pl
from jax.experimental.pallas import tpu as pltpu
from jax.sharding import PartitionSpec as P

F32, BF16 = jnp.float32, jnp.bfloat16
VMEM_LIMIT = 12 << 20
LANES = 128


def shifted(shard, axis, by):
    count = lax.axis_size(axis)
    pairs = [(i, i + by) for i in range(count) if 0 <= i + by < count]
    return lax.ppermute(shard, axis, pairs)


def short_conv(values, taps, rim):
    tap_count = taps.shape[1]
    length = values.shape[1]
    padded = jnp.concatenate([rim, values], axis=1)
    total = jnp.zeros_like(values)
    for k in range(tap_count):
        total = (
            total + taps[:, k : k + 1] * padded[:, tap_count - 1 - k : tap_count - 1 - k + length]
        )
    return total


def dft_tables(height, breadth, period):
    rindex = lax.broadcasted_iota(jnp.int32, (height, breadth), 0)
    cindex = lax.broadcasted_iota(jnp.int32, (height, breadth), 1)
    phase_angle = (rindex * cindex % period).astype(F32) * (2.0 * math.pi / period)
    return (jnp.cos(phase_angle), jnp.sin(phase_angle))


def split_table(table):
    upper = table.astype(BF16)
    lower = (table - upper.astype(F32)).astype(BF16)
    return (upper, lower)


def precise(pattern, left_op, right_op):
    return jnp.einsum(pattern, left_op, right_op, precision=lax.Precision.HIGHEST)


def narrow(pattern, parts, right_op):
    first = jnp.einsum(pattern, parts[0], right_op, preferred_element_type=F32)
    return first + jnp.einsum(pattern, parts[1], right_op, preferred_element_type=F32)


def make_tables(length):
    breadth = 128
    height = 2 * length // breadth
    row_tables = dft_tables(height, height // 2, height)
    twist_tables = dft_tables(height, breadth, 2 * length)
    col_tables = dft_tables(breadth, breadth, breadth)
    row_split = (split_table(row_tables[0]), split_table(row_tables[1]))
    return (row_tables, twist_tables, col_tables, row_split)


def forward_dft(values, tables):
    row_tables, twist_tables, col_tables, row_split = tables
    chan_count, length = values.shape
    folded = values.reshape(chan_count, length // 128, 128)
    first_re = narrow("kp,cpq->ckq", row_split[0], folded)
    first_im = -narrow("kp,cpq->ckq", row_split[1], folded)
    turned_re = first_re * twist_tables[0] + first_im * twist_tables[1]
    turned_im = first_im * twist_tables[0] - first_re * twist_tables[1]
    spec_re = precise("ckq,qm->ckm", turned_re, col_tables[0]) + precise(
        "ckq,qm->ckm", turned_im, col_tables[1]
    )
    spec_im = precise("ckq,qm->ckm", turned_im, col_tables[0]) - precise(
        "ckq,qm->ckm", turned_re, col_tables[1]
    )
    return (spec_re, spec_im)


def inverse_dft(spec_re, spec_im, tables, length):
    row_tables, twist_tables, col_tables, row_split = tables
    chan_count = spec_re.shape[0]
    back_re = precise("ckm,mq->ckq", spec_re, col_tables[0]) - precise(
        "ckm,mq->ckq", spec_im, col_tables[1]
    )
    back_im = precise("ckm,mq->ckq", spec_re, col_tables[1]) + precise(
        "ckm,mq->ckq", spec_im, col_tables[0]
    )
    twist_re = back_re * twist_tables[0] - back_im * twist_tables[1]
    twist_im = back_re * twist_tables[1] + back_im * twist_tables[0]
    folded = precise("kp,ckq->cpq", row_tables[0], twist_re) - precise(
        "kp,ckq->cpq", row_tables[1], twist_im
    )
    return (folded / (2.0 * length)).reshape(chan_count, length)


def long_mix(gated_narrow, kernel, bypass):
    length = gated_narrow.shape[1]
    tables = make_tables(length)
    kern_re, kern_im = forward_dft(kernel, tables)
    sig_re, sig_im = forward_dft(gated_narrow, tables)
    prod_re = sig_re * kern_re - sig_im * kern_im
    prod_im = sig_re * kern_im + sig_im * kern_re
    return inverse_dft(prod_re, prod_im, tables, length) + bypass[:, None] * gated_narrow.astype(
        F32
    )


def general_path(signal, input_gate, output_gate, short_taps, long_filter, bypass_gain):
    channels, local_tokens = signal.shape
    rim_len = short_taps.shape[2] - 1
    taps = short_taps.astype(F32)
    feats = []
    for i, stream in enumerate((signal, input_gate, output_gate)):
        rim = shifted(stream[:, local_tokens - rim_len :], "ctx", 1)
        feats.append(short_conv(stream.astype(F32), taps[i], rim.astype(F32)))
    gated = (feats[1] * feats[0]).astype(BF16)
    gated = lax.all_to_all(gated, "ctx", split_axis=0, concat_axis=1, tiled=True)
    longconv = long_mix(gated, long_filter, bypass_gain).astype(BF16)
    returned = lax.all_to_all(longconv, "ctx", split_axis=1, concat_axis=0, tiled=True)
    return (feats[2] * returned.astype(F32)).astype(BF16)


def add(a, b):
    return b if a is None else a if b is None else a + b


def sub(a, b):
    return a if b is None else -b if a is None else a - b


def turn(value, k, n):
    re, im = value
    k %= n
    if k == 0:
        return value
    if 4 * k == n:
        return (None if im is None else -im, re)
    if 4 * k == 3 * n:
        return (im, None if re is None else -re)
    c, s = math.cos(2 * math.pi * k / n), math.sin(2 * math.pi * k / n)
    if im is None:
        return (re * c, re * s)
    if re is None:
        return (im * -s, im * c)
    return (re * c - im * s, re * s + im * c)


def rfft(xs):
    n = len(xs)
    if n == 1:
        return [(xs[0], None)]
    half = n // 2
    even, odd = rfft(xs[0::2]), rfft(xs[1::2])
    out = [None] * (half + 1)
    for k in range(half // 2 + 1):
        e, t = even[k], turn(odd[k], -k, n)
        out[k] = (add(e[0], t[0]), add(e[1], t[1]))
        if half - k != k:
            out[half - k] = (sub(e[0], t[0]), sub(t[1], e[1]))
    return out


def irfft_first_half(zs):
    half = len(zs) - 1
    n = 2 * half
    if n == 2:
        return [add(zs[0][0], zs[1][0])]
    even, odd = [], []
    for k in range(half // 2 + 1):
        a, b = zs[k], zs[half - k]
        if k == half - k:
            even.append((a[0] * 2.0, None))
            odd.append((a[1] * -2.0, None))
            continue
        even.append((add(a[0], b[0]), sub(a[1], b[1])))
        odd.append(turn((sub(a[0], b[0]), add(a[1], b[1])), k, n))
    first, second = irfft_first_half(even), irfft_first_half(odd)
    return [v for pair in zip(first, second) for v in pair]


def hi_lo(value):
    upper = value.astype(BF16)
    return upper, (value - upper.astype(F32)).astype(BF16)


def transform_bases(blocks, inner):
    index = np.arange(inner)
    angle = 2 * np.pi * (np.outer(index, index) % inner) / inner
    turns = np.pi * np.outer(np.arange(blocks + 1), index) / (blocks * inner)
    return [
        jnp.asarray(np.stack([np.cos(x), np.sin(x)]).astype(np.float32)) for x in (angle, turns)
    ]


def table_kernel(base_ref, turn_ref, fwd_ref, bwd_ref):
    inner = base_ref.shape[1]
    scale = 1.0 / (2 * (turn_ref.shape[1] - 1) * inner)
    base_c, base_s = base_ref[0], base_ref[1]

    def step(k, carry):
        tc, ts = turn_ref[0, pl.ds(k, 1), :], turn_ref[1, pl.ds(k, 1), :]
        c, s = base_c * tc - base_s * ts, base_s * tc + base_c * ts
        back_c, back_s = c.T * scale, s.T * scale
        for ref, cos, up, down in ((fwd_ref, c, s, -s), (bwd_ref, back_c, -back_s, back_s)):
            for part in (0, 1):
                for row, col, value in ((0, 0, cos), (0, 1, up), (1, 0, down), (1, 1, cos)):
                    ref[
                        k,
                        pl.ds(row * inner, inner),
                        pl.ds((2 * part + col) * inner, inner),
                    ] = hi_lo(value)[part]
        return carry

    lax.fori_loop(0, fwd_ref.shape[0], step, 0)


ROWS = 16


def over_tiles(rows, lanes, body):
    lane_tiles = lanes // LANES

    def step(t, carry):
        body(
            pl.multiple_of(t // lane_tiles * ROWS, ROWS),
            pl.multiple_of(t % lane_tiles * LANES, LANES),
        )
        return carry

    lax.fori_loop(0, rows // ROWS * lane_tiles, step, 0, unroll=2)


def outer_forward(src_ref, hi_ref, lo_ref):
    blocks, inner, chans = src_ref.shape

    def tile(row, lane):
        xs = [src_ref[b, pl.ds(row, ROWS), pl.ds(lane, LANES)].astype(F32) for b in range(blocks)]
        for k, (re, im) in enumerate(rfft(xs + [None] * blocks)):
            if im is None:
                im = jnp.zeros_like(re)
            for part, base in ((re, 0), (im, inner)):
                upper, lower = hi_lo(part)
                hi_ref[k, pl.ds(base + row, ROWS), pl.ds(lane, LANES)] = upper
                lo_ref[k, pl.ds(base + row, ROWS), pl.ds(lane, LANES)] = lower

    over_tiles(inner, chans, tile)


def inner_product(table, upper, lower):
    width = table.shape[1] // 2
    table = jnp.concatenate([table[:, :width], table], axis=1)
    stacked = jnp.concatenate([lower, upper, upper], axis=0)
    return jnp.dot(table, stacked, preferred_element_type=F32)


def spectrum_kernel(filt_ref, gain_ref, fwd_ref, spec_ref, hi_ref, lo_ref):
    outer_forward(filt_ref, hi_ref, lo_ref)
    inner = filt_ref.shape[1]
    gain = gain_ref[...]
    for k in range(spec_ref.shape[0]):
        spec = inner_product(fwd_ref[k], hi_ref[k], lo_ref[k])
        spec_ref[k, :inner] = spec[:inner] + gain
        spec_ref[k, inner:] = spec[inner:]


def conv_kernel(
    gated_ref, spec_any, fwd_any, bwd_any, out_ref, hi_ref, lo_ref, back_ref, spec_ref, fwd_ref,
    bwd_ref, sems
):
    blocks, inner, chans = gated_ref.shape
    freqs = blocks + 1
    cuts = [0, freqs // 2, freqs]
    copies = [
        [
            pltpu.make_async_copy(
                src.at[pl.ds(lo, hi - lo)], dst.at[pl.ds(lo, hi - lo)], sems.at[part, i]
            )
            for i, (src, dst) in enumerate(
                ((spec_any, spec_ref), (fwd_any, fwd_ref), (bwd_any, bwd_ref))
            )
        ]
        for part, (lo, hi) in enumerate(zip(cuts, cuts[1:]))
    ]
    for part in copies:
        for copy in part:
            copy.start()
    outer_forward(gated_ref, hi_ref, lo_ref)
    for part, (lo, hi) in enumerate(zip(cuts, cuts[1:])):
        for copy in copies[part]:
            copy.wait()
        for k in range(lo, hi):
            sig = inner_product(fwd_ref[k], hi_ref[k], lo_ref[k])
            sig_re, sig_im = sig[:inner], sig[inner:]
            ker_re, ker_im = spec_ref[k, :inner], spec_ref[k, inner:]
            prod = jnp.concatenate(
                [sig_re * ker_re - sig_im * ker_im, sig_re * ker_im + sig_im * ker_re], axis=0
            )
            back_ref[k] = inner_product(bwd_ref[k], *hi_lo(prod))

    def tile(row, lane):
        zs = []
        for k in range(freqs):
            re = back_ref[k, pl.ds(row, ROWS), pl.ds(lane, LANES)]
            im = None
            if 0 < k < blocks:
                im = back_ref[k, pl.ds(inner + row, ROWS), pl.ds(lane, LANES)]
            zs.append((re, im))
        for b, value in enumerate(irfft_first_half(zs)):
            out_ref[b, pl.ds(row, ROWS), pl.ds(lane, LANES)] = value.astype(BF16)

    over_tiles(inner, chans, tile)


def cost(flops, size):
    return pl.CostEstimate(flops=flops, bytes_accessed=size, transcendentals=0)


def transform_tables(blocks, inner):
    shape = jax.ShapeDtypeStruct((blocks + 1, 2 * inner, 4 * inner), BF16)
    return pl.pallas_call(
        table_kernel,
        out_shape=[shape, shape],
        compiler_params=pltpu.CompilerParams(vmem_limit_bytes=12 << 20),
        cost_estimate=cost(2 * 10**9, 9 << 20),
        name="transform_tables",
    )(*transform_bases(blocks, inner))


def filter_spectrum(filt, gain, forward):
    blocks, inner, chans = filt.shape
    return pl.pallas_call(
        spectrum_kernel,
        out_shape=jax.ShapeDtypeStruct((blocks + 1, 2 * inner, chans), F32),
        scratch_shapes=[pltpu.VMEM((blocks + 1, 2 * inner, chans), BF16)] * 2,
        compiler_params=pltpu.CompilerParams(vmem_limit_bytes=20 << 20),
        cost_estimate=cost(4 * 10**9, 8 << 20),
        name="filter_spectrum",
    )(filt, gain, forward)


def long_conv(gated, spectrum, forward, backward):
    blocks, inner, chans = gated.shape
    freqs = blocks + 1
    spec_shape, table_shape = spectrum.shape, forward.shape
    vmem, hbm = (pl.BlockSpec(memory_space=m) for m in (pltpu.VMEM, pl.ANY))
    return pl.pallas_call(
        conv_kernel,
        in_specs=[vmem, hbm, hbm, hbm],
        out_specs=vmem,
        out_shape=jax.ShapeDtypeStruct(gated.shape, BF16),
        scratch_shapes=[pltpu.VMEM(spec_shape, BF16)] * 2
        + [pltpu.VMEM(spec_shape, F32)] * 2
        + [pltpu.VMEM(table_shape, BF16)] * 2
        + [pltpu.SemaphoreType.DMA((2, 3))],
        compiler_params=pltpu.CompilerParams(vmem_limit_bytes=30 << 20),
        cost_estimate=cost(8 * 10**9, 8 << 20),
        name="long_conv",
    )(gated, spectrum, forward, backward)


PAD = 8


def short_sum(pad_ref, taps_ref, lane, rows):
    total = None
    for k in range(taps_ref.shape[0]):
        term = taps_ref[k : k + 1, pl.ds(lane, LANES)] * pad_ref[pl.ds(PAD - k, rows), :]
        total = term if total is None else total + term
    return total


def in_hbm(x):
    return pltpu.with_memory_space_constraint(x, pltpu.HBM)


def tail_kernel(*refs):
    out_ref = refs[-1]
    for i, ref in enumerate(refs[:-1]):
        for lane in range(0, ref.shape[0], LANES):
            turned = ref[pl.ds(lane, LANES), :].T
            out_ref[pl.ds(i * PAD, PAD), pl.ds(lane, LANES)] = turned[-PAD:]


PIECES = 4


def take_kernel(sig_any, key_any, taps_any, rim_ref, held_ref, wide_ref, taps_ref, sems, tap_sem):
    size = held_ref.shape[1] // PIECES
    copies = [
        [
            pltpu.make_async_copy(
                src.at[pl.ds(p * size, size), :],
                held_ref.at[i, pl.ds(p * size, size), :],
                sems.at[i, p],
            )
            for i, src in enumerate((sig_any, key_any))
        ]
        for p in range(PIECES)
    ]
    tap_copy = pltpu.make_async_copy(taps_any, taps_ref, tap_sem)
    for piece in copies:
        for copy in piece:
            copy.start()
    tap_copy.start()
    for p, piece in enumerate(copies):
        for i, copy in enumerate(piece):
            copy.wait()
            for lane in range(p * size, (p + 1) * size, LANES):
                turned = held_ref[i, pl.ds(lane, LANES), :].T
                rim_ref[pl.ds(i * PAD, PAD), pl.ds(lane, LANES)] = turned[-PAD:]
    tap_copy.wait()
    wide_ref[...] = taps_ref[...].astype(F32)


def gate_kernel(held_ref, taps_ref, out_ref, head_ref, pad_ref):
    rows, chans = out_ref.shape[1:]
    pad_ref[:, :PAD] = jnp.zeros((2, PAD, LANES), F32)
    for lane in range(0, held_ref.shape[1], LANES):
        feats = []
        for i in range(2):
            turned = held_ref[i, pl.ds(lane, LANES), :].T.astype(F32)
            pad_ref[i, pl.ds(PAD, rows), :] = turned
            head_ref[i, :, pl.ds(lane, LANES)] = turned[:ROWS]
            feats.append(short_sum(pad_ref.at[i], taps_ref.at[i], lane, rows))
        out_ref[lane // chans, :, pl.ds(lane % chans, LANES)] = (feats[1] * feats[0]).astype(BF16)


def rim_kernel(head_ref, rim_ref, taps_ref, whole_ref, out_ref, pad_ref):
    blocks, rows, chans = out_ref.shape
    for lane in range(0, blocks * chans, LANES):
        feats = []
        for i in range(2):
            pad_ref[i, :PAD] = rim_ref[pl.ds(i * PAD, PAD), pl.ds(lane, LANES)].astype(F32)
            pad_ref[i, PAD:] = head_ref[i, :, pl.ds(lane, LANES)]
            feats.append(short_sum(pad_ref.at[i], taps_ref.at[i], lane, rows))
        out_ref[lane // chans, :, pl.ds(lane % chans, LANES)] = (feats[1] * feats[0]).astype(BF16)


def query_kernel(query_ref, rim_ref, taps_ref, out_ref, pad_ref):
    rows, chans = out_ref.shape[1:]
    for lane in range(0, query_ref.shape[0], LANES):
        pad_ref[:PAD] = rim_ref[:, pl.ds(lane, LANES)].astype(F32)
        pad_ref[PAD:] = query_ref[pl.ds(lane, LANES), :].T.astype(F32)
        out_ref[lane // chans, :, pl.ds(lane % chans, LANES)] = short_sum(
            pad_ref, taps_ref.at[2], lane, rows
        )


def mix_kernel(conv_ref, query_ref, out_ref):
    blocks, rows, chans = conv_ref.shape
    for lane in range(0, blocks * chans, LANES):
        here = (lane // chans, slice(None), pl.ds(lane % chans, LANES))
        value = conv_ref[here].astype(F32) * query_ref[here]
        out_ref[pl.ds(lane, LANES), :] = value.astype(BF16).T


def fast_path(signal, input_gate, output_gate, short_taps, long_filter, bypass_gain):
    channels, rows = signal.shape
    tap_count = short_taps.shape[2]
    chans, length = long_filter.shape
    blocks = length // rows
    taps = short_taps.transpose(0, 2, 1)
    params = pltpu.CompilerParams(vmem_limit_bytes=VMEM_LIMIT)
    some, most = max(blocks // 4, 1), max(blocks // 2, 1)

    def stream_spec(count):
        return pl.BlockSpec((count * chans, rows), lambda i: (i, 0))

    def block_spec(count):
        return pl.BlockSpec((count, rows, chans), lambda i: (i, 0, 0))

    def taps_spec(count):
        return pl.BlockSpec((3, tap_count, count * chans), lambda i: (0, 0, i))

    def whole(shape):
        return pl.BlockSpec(shape, lambda i: (0,) * len(shape))

    vmem, hbm = (pl.BlockSpec(memory_space=m) for m in (pltpu.VMEM, pl.ANY))
    last, held, wide = pl.pallas_call(
        take_kernel,
        in_specs=[hbm] * 3,
        out_specs=[vmem] * 3,
        out_shape=[
            jax.ShapeDtypeStruct((2 * PAD, channels), BF16),
            jax.ShapeDtypeStruct((2, channels, rows), BF16),
            jax.ShapeDtypeStruct(taps.shape, F32),
        ],
        scratch_shapes=[
            pltpu.VMEM(taps.shape, BF16),
            pltpu.SemaphoreType.DMA((2, PIECES)),
            pltpu.SemaphoreType.DMA,
        ],
        compiler_params=params,
        cost_estimate=cost(10**8, 4 << 20),
        name="take",
    )(in_hbm(signal), in_hbm(input_gate), in_hbm(taps))
    rim = shifted(last, "ctx", 1)
    gated, head = pl.pallas_call(
        gate_kernel,
        grid=(blocks // some,),
        in_specs=[
            pl.BlockSpec((2, some * chans, rows), lambda i: (0, i, 0)),
            taps_spec(some),
        ],
        out_specs=[block_spec(some), pl.BlockSpec((2, ROWS, some * chans), lambda i: (0, 0, i))],
        out_shape=[
            jax.ShapeDtypeStruct((blocks, rows, chans), BF16),
            jax.ShapeDtypeStruct((2, ROWS, channels), F32),
        ],
        scratch_shapes=[pltpu.VMEM((2, PAD + rows, LANES), F32)],
        compiler_params=params,
        cost_estimate=cost(10**9, 8 << 20),
        name="gate_main",
    )(held, wide)
    gated = pl.pallas_call(
        rim_kernel,
        grid=(1,),
        in_specs=[
            whole((2, ROWS, channels)),
            whole((2 * PAD, channels)),
            whole((3, tap_count, channels)),
            pl.BlockSpec(memory_space=pl.ANY),
        ],
        out_specs=whole((blocks, ROWS, chans)),
        out_shape=jax.ShapeDtypeStruct((blocks, rows, chans), BF16),
        scratch_shapes=[pltpu.VMEM((2, PAD + ROWS, LANES), F32)],
        input_output_aliases={3: 0},
        compiler_params=params,
        cost_estimate=cost(10**7, 1 << 20),
        name="gate_rim",
    )(head, rim, wide, gated)
    arrived = lax.all_to_all(gated, "ctx", 0, 0)

    forward, backward = transform_tables(blocks, rows)
    filt = long_filter.reshape(chans, blocks, rows).transpose(1, 2, 0)
    spectrum = filter_spectrum(filt, bypass_gain.reshape(1, chans), forward)
    query_last = pl.pallas_call(
        tail_kernel,
        out_shape=jax.ShapeDtypeStruct((PAD, channels), BF16),
        compiler_params=params,
        cost_estimate=cost(10**8, 2 << 20),
        name="query_last",
    )(output_gate)
    query_rim = shifted(query_last, "ctx", 1)
    query = pl.pallas_call(
        query_kernel,
        grid=(blocks // some,),
        in_specs=[
            stream_spec(some),
            pl.BlockSpec((PAD, some * chans), lambda i: (0, i)),
            taps_spec(some),
        ],
        out_specs=block_spec(some),
        out_shape=jax.ShapeDtypeStruct((blocks, rows, chans), F32),
        scratch_shapes=[pltpu.VMEM((PAD + rows, LANES), F32)],
        compiler_params=params,
        cost_estimate=cost(10**9, 8 << 20),
        name="query_feat",
    )(output_gate, query_rim, wide)

    conv = long_conv(arrived, in_hbm(spectrum), in_hbm(forward), in_hbm(backward))
    returned = lax.all_to_all(conv, "ctx", 0, 0)
    return pl.pallas_call(
        mix_kernel,
        grid=(blocks // most,),
        in_specs=[block_spec(most), block_spec(most)],
        out_specs=stream_spec(most),
        out_shape=jax.ShapeDtypeStruct((channels, rows), BF16),
        compiler_params=params,
        cost_estimate=cost(10**8, 4 << 20),
        name="mix",
    )(returned, query)


def on_device(signal, input_gate, output_gate, short_taps, long_filter, bypass_gain):
    channels, rows = signal.shape
    chans, length = long_filter.shape
    blocks = length // rows
    fits = (
        rows == LANES
        and chans % LANES == 0
        and chans * blocks == channels
        and blocks * rows == length
        and blocks in (2, 4, 8, 16)
        and short_taps.shape[2] <= PAD
    )
    path = fast_path if fits else general_path
    return path(signal, input_gate, output_gate, short_taps, long_filter, bypass_gain)


def solution(mesh):
    placed = (
        P(None, ("groups", "ctx")),
        P(None, ("groups", "ctx")),
        P(None, ("groups", "ctx")),
        P(),
        P("ctx", None),
        P("ctx"),
    )
    return jax.shard_map(
        on_device, mesh=mesh, in_specs=placed, out_specs=P(None, ("groups", "ctx")), check_vma=False
    )
```

```python
import functools
import math

import jax
import jax.numpy as jnp
import numpy as np
from jax import lax
from jax.experimental import pallas as pl
from jax.experimental.pallas import tpu as pltpu
from jax.sharding import PartitionSpec as P

F32, BF16 = jnp.float32, jnp.bfloat16
VMEM_LIMIT = 12 << 20
LANES = 128


def shifted(shard, axis, by):
    count = lax.axis_size(axis)
    pairs = [(i, i + by) for i in range(count) if 0 <= i + by < count]
    return lax.ppermute(shard, axis, pairs)


def short_conv(values, taps, rim):
    tap_count = taps.shape[1]
    length = values.shape[1]
    padded = jnp.concatenate([rim, values], axis=1)
    total = jnp.zeros_like(values)
    for k in range(tap_count):
        total = (
            total + taps[:, k : k + 1] * padded[:, tap_count - 1 - k : tap_count - 1 - k + length]
        )
    return total


def dft_tables(height, breadth, period):
    rindex = lax.broadcasted_iota(jnp.int32, (height, breadth), 0)
    cindex = lax.broadcasted_iota(jnp.int32, (height, breadth), 1)
    phase_angle = (rindex * cindex % period).astype(F32) * (2.0 * math.pi / period)
    return (jnp.cos(phase_angle), jnp.sin(phase_angle))


def split_table(table):
    upper = table.astype(BF16)
    lower = (table - upper.astype(F32)).astype(BF16)
    return (upper, lower)


def precise(pattern, left_op, right_op):
    return jnp.einsum(pattern, left_op, right_op, precision=lax.Precision.HIGHEST)


def narrow(pattern, parts, right_op):
    first = jnp.einsum(pattern, parts[0], right_op, preferred_element_type=F32)
    return first + jnp.einsum(pattern, parts[1], right_op, preferred_element_type=F32)


def make_tables(length):
    breadth = 128
    height = 2 * length // breadth
    row_tables = dft_tables(height, height // 2, height)
    twist_tables = dft_tables(height, breadth, 2 * length)
    col_tables = dft_tables(breadth, breadth, breadth)
    row_split = (split_table(row_tables[0]), split_table(row_tables[1]))
    return (row_tables, twist_tables, col_tables, row_split)


def forward_dft(values, tables):
    row_tables, twist_tables, col_tables, row_split = tables
    chan_count, length = values.shape
    folded = values.reshape(chan_count, length // 128, 128)
    first_re = narrow("kp,cpq->ckq", row_split[0], folded)
    first_im = -narrow("kp,cpq->ckq", row_split[1], folded)
    turned_re = first_re * twist_tables[0] + first_im * twist_tables[1]
    turned_im = first_im * twist_tables[0] - first_re * twist_tables[1]
    spec_re = precise("ckq,qm->ckm", turned_re, col_tables[0]) + precise(
        "ckq,qm->ckm", turned_im, col_tables[1]
    )
    spec_im = precise("ckq,qm->ckm", turned_im, col_tables[0]) - precise(
        "ckq,qm->ckm", turned_re, col_tables[1]
    )
    return (spec_re, spec_im)


def inverse_dft(spec_re, spec_im, tables, length):
    row_tables, twist_tables, col_tables, row_split = tables
    chan_count = spec_re.shape[0]
    back_re = precise("ckm,mq->ckq", spec_re, col_tables[0]) - precise(
        "ckm,mq->ckq", spec_im, col_tables[1]
    )
    back_im = precise("ckm,mq->ckq", spec_re, col_tables[1]) + precise(
        "ckm,mq->ckq", spec_im, col_tables[0]
    )
    twist_re = back_re * twist_tables[0] - back_im * twist_tables[1]
    twist_im = back_re * twist_tables[1] + back_im * twist_tables[0]
    folded = precise("kp,ckq->cpq", row_tables[0], twist_re) - precise(
        "kp,ckq->cpq", row_tables[1], twist_im
    )
    return (folded / (2.0 * length)).reshape(chan_count, length)


def long_mix(gated_narrow, kernel, bypass):
    length = gated_narrow.shape[1]
    tables = make_tables(length)
    kern_re, kern_im = forward_dft(kernel, tables)
    sig_re, sig_im = forward_dft(gated_narrow, tables)
    prod_re = sig_re * kern_re - sig_im * kern_im
    prod_im = sig_re * kern_im + sig_im * kern_re
    return inverse_dft(prod_re, prod_im, tables, length) + bypass[:, None] * gated_narrow.astype(
        F32
    )


def general_path(signal, input_gate, output_gate, short_taps, long_filter, bypass_gain):
    channels, local_tokens = signal.shape
    rim_len = short_taps.shape[2] - 1
    taps = short_taps.astype(F32)
    feats = []
    for i, stream in enumerate((signal, input_gate, output_gate)):
        rim = shifted(stream[:, local_tokens - rim_len :], "ctx", 1)
        feats.append(short_conv(stream.astype(F32), taps[i], rim.astype(F32)))
    gated = (feats[1] * feats[0]).astype(BF16)
    gated = lax.all_to_all(gated, "ctx", split_axis=0, concat_axis=1, tiled=True)
    longconv = long_mix(gated, long_filter, bypass_gain).astype(BF16)
    returned = lax.all_to_all(longconv, "ctx", split_axis=1, concat_axis=0, tiled=True)
    return (feats[2] * returned.astype(F32)).astype(BF16)


def add(a, b):
    return b if a is None else a if b is None else a + b


def sub(a, b):
    return a if b is None else -b if a is None else a - b


def turn(value, k, n):
    re, im = value
    k %= n
    if k == 0:
        return value
    if 4 * k == n:
        return (None if im is None else -im, re)
    if 4 * k == 3 * n:
        return (im, None if re is None else -re)
    c, s = math.cos(2 * math.pi * k / n), math.sin(2 * math.pi * k / n)
    if im is None:
        return (re * c, re * s)
    if re is None:
        return (im * -s, im * c)
    return (re * c - im * s, re * s + im * c)


def rfft(xs):
    n = len(xs)
    if n == 1:
        return [(xs[0], None)]
    half = n // 2
    even, odd = rfft(xs[0::2]), rfft(xs[1::2])
    out = [None] * (half + 1)
    for k in range(half // 2 + 1):
        e, t = even[k], turn(odd[k], -k, n)
        out[k] = (add(e[0], t[0]), add(e[1], t[1]))
        if half - k != k:
            out[half - k] = (sub(e[0], t[0]), sub(t[1], e[1]))
    return out


def irfft_first_half(zs):
    half = len(zs) - 1
    n = 2 * half
    if n == 2:
        return [add(zs[0][0], zs[1][0])]
    even, odd = [], []
    for k in range(half // 2 + 1):
        a, b = zs[k], zs[half - k]
        if k == half - k:
            even.append((a[0] * 2.0, None))
            odd.append((a[1] * -2.0, None))
            continue
        even.append((add(a[0], b[0]), sub(a[1], b[1])))
        odd.append(turn((sub(a[0], b[0]), add(a[1], b[1])), k, n))
    first, second = irfft_first_half(even), irfft_first_half(odd)
    return [v for pair in zip(first, second) for v in pair]


def hi_lo(value):
    upper = value.astype(BF16)
    return upper, (value - upper.astype(F32)).astype(BF16)


def np_hi_lo(table):
    table = table.astype(np.float32)
    upper = table.astype(jnp.bfloat16)
    return [upper, (table - upper.astype(np.float32)).astype(jnp.bfloat16)]


def transform_tables(blocks, inner):
    index = np.arange(inner)
    angle = 2 * np.pi * (np.outer(index, index) % inner) / inner
    c, s = np.cos(angle), np.sin(angle)
    turns = np.pi * np.outer(np.arange(blocks + 1), index) / (blocks * inner)
    forward, backward = (
        jnp.asarray(np.concatenate([upper, upper, lower]))
        for upper, lower in (
            np_hi_lo(np.block([[c, -s], [s, c]])),
            np_hi_lo(np.block([[c, s], [-s, c]]) / (2 * blocks * inner)),
        )
    )
    return forward, backward, jnp.asarray(np.stack([np.cos(turns), np.sin(turns)]), F32)


ROWS = 16


def over_rows(rows, body):
    def step(t, carry):
        body(pl.multiple_of(t * ROWS, ROWS))
        return carry

    lax.fori_loop(0, rows // ROWS, step, 0, unroll=2)


def outer_forward(load, blocks, turn_ref, hi_ref, lo_ref):
    freqs, chans, width = hi_ref.shape
    inner = width // 2

    def tile(row):
        xs = [load(b, row).astype(F32) for b in range(blocks)]
        for k, (re, im) in enumerate(rfft(xs + [None] * blocks)):
            if k:
                c, s = turn_ref[0, k : k + 1, :], turn_ref[1, k : k + 1, :]
                if im is None:
                    re, im = re * c, -(re * s)
                else:
                    re, im = re * c + im * s, im * c - re * s
            if im is None:
                im = jnp.zeros_like(re)
            for part, base in ((re, 0), (im, inner)):
                upper, lower = hi_lo(part)
                hi_ref[k, pl.ds(row, ROWS), pl.ds(base, inner)] = upper
                lo_ref[k, pl.ds(row, ROWS), pl.ds(base, inner)] = lower

    over_rows(chans, tile)


def inner_product(upper, lower, table_ref):
    stacked = jnp.concatenate([upper, lower, upper], axis=1)
    return jnp.dot(stacked, table_ref[...], preferred_element_type=F32)


def groups_of(count, size):
    return [range(k, min(k + size, count)) for k in range(0, count, size)]


STACK = 2
TILE = 16


def stacked_rows(ref, ks):
    return ref[ks[0] : ks[-1] + 1].reshape(len(ks) * ref.shape[1], ref.shape[2])


def spectrum_kernel(filt_ref, gain_ref, turn_ref, fwd_ref, spec_ref, hi_ref, lo_ref):
    chans = filt_ref.shape[0]
    inner = hi_ref.shape[2] // 2
    blocks = hi_ref.shape[0] - 1
    outer_forward(
        lambda b, row: filt_ref[pl.ds(row, ROWS), b * inner : (b + 1) * inner],
        blocks,
        turn_ref,
        hi_ref,
        lo_ref,
    )
    gain = gain_ref[...]
    for ks in groups_of(blocks + 1, STACK):
        spec = inner_product(stacked_rows(hi_ref, ks), stacked_rows(lo_ref, ks), fwd_ref)
        for i, k in enumerate(ks):
            part = spec[i * chans : (i + 1) * chans]
            spec_ref[k, :, :inner] = part[:, :inner] + gain
            spec_ref[k, :, inner:] = part[:, inner:]


def conv_kernel(
    gated_ref, spec_any, turn_any, fwd_any, bwd_any, out_ref, turned_ref, hi_ref, lo_ref, back_ref,
    spec_ref, turn_ref, fwd_ref, bwd_ref, sems
):
    blocks, inner, chans = gated_ref.shape
    freqs = blocks + 1
    tiles = chans // TILE
    copies = [
        pltpu.make_async_copy(src, dst, sems.at[i])
        for i, (src, dst) in enumerate(
            (
                (turn_any, turn_ref),
                (fwd_any, fwd_ref),
                (bwd_any, bwd_ref),
                (spec_any.at[:, : chans // 2], spec_ref.at[:, : chans // 2]),
                (spec_any.at[:, chans // 2 :], spec_ref.at[:, chans // 2 :]),
            )
        )
    ]
    for copy in copies:
        copy.start()
    for b in range(blocks):
        turned_ref[b] = gated_ref[b].T
    copies[0].wait()

    def outer(t):
        def tile(row):
            xs = [turned_ref[b, t * TILE + row : t * TILE + row + ROWS].astype(F32) for b in range(blocks)]
            for k, (re, im) in enumerate(rfft(xs + [None] * blocks)):
                if k:
                    c, s = turn_ref[0, k : k + 1, :], turn_ref[1, k : k + 1, :]
                    if im is None:
                        re, im = re * c, -(re * s)
                    else:
                        re, im = re * c + im * s, im * c - re * s
                if im is None:
                    im = jnp.zeros_like(re)
                for part, base in ((re, 0), (im, inner)):
                    upper, lower = hi_lo(part)
                    hi_ref[t % 2, k, row : row + ROWS, base : base + inner] = upper
                    lo_ref[t % 2, k, row : row + ROWS, base : base + inner] = lower

        for row in range(0, TILE, ROWS):
            tile(row)

    def flat(x):
        return x.reshape(freqs * TILE, 2 * inner)

    def inverse(t):
        for row in range(0, TILE, ROWS):
            zs = []
            for k in range(freqs):
                re = back_ref[t % 2, k, row : row + ROWS, :inner]
                if k == 0:
                    zs.append((re, None))
                    continue
                im = back_ref[t % 2, k, row : row + ROWS, inner:]
                c, s = turn_ref[0, k : k + 1, :], turn_ref[1, k : k + 1, :]
                zs.append((re * c - im * s, None if k == blocks else re * s + im * c))
            for b, value in enumerate(irfft_first_half(zs)):
                out_ref[b, t * TILE + row : t * TILE + row + ROWS, :] = value.astype(BF16)

    outer(0)
    copies[1].wait()
    copies[2].wait()
    for t in range(tiles):
        if t in (0, tiles // 2):
            copies[3 if t == 0 else 4].wait()
        sig = inner_product(flat(hi_ref[t % 2]), flat(lo_ref[t % 2]), fwd_ref)
        if t + 1 < tiles:
            outer(t + 1)
        ker = flat(spec_ref[:, t * TILE : (t + 1) * TILE])
        sig_re, sig_im, ker_re, ker_im = (
            x[:, at : at + inner] for x in (sig, ker) for at in (0, inner)
        )
        prod = jnp.concatenate(
            [sig_re * ker_re - sig_im * ker_im, sig_re * ker_im + sig_im * ker_re], axis=1
        )
        back = inner_product(*hi_lo(prod), bwd_ref)
        back_ref[t % 2] = back.reshape(freqs, TILE, 2 * inner)
        if t:
            inverse(t - 1)
    inverse(tiles - 1)


def cost(flops, size):
    return pl.CostEstimate(flops=flops, bytes_accessed=size, transcendentals=0)


def whole(shape):
    return pl.BlockSpec(shape, lambda i: (0,) * len(shape))


def filter_spectrum(filt, gain, tables, blocks):
    forward, _, turns = tables
    chans, inner = filt.shape[0], filt.shape[1] // blocks
    shape = (blocks + 1, chans, 2 * inner)
    return pl.pallas_call(
        spectrum_kernel,
        out_shape=jax.ShapeDtypeStruct(shape, F32),
        scratch_shapes=[pltpu.VMEM(shape, BF16)] * 2,
        compiler_params=pltpu.CompilerParams(vmem_limit_bytes=20 << 20),
        cost_estimate=cost(3 * 10**9, 4 << 20),
        name="filter_spectrum",
    )(filt, gain, turns, forward)


def long_conv(gated, spectrum, tables):
    forward, backward, turns = tables
    blocks, inner, chans = gated.shape
    tile = (2, blocks + 1, TILE, 2 * inner)
    operands = [in_hbm(x) for x in (spectrum, turns, forward, backward)]
    vmem, hbm = (pl.BlockSpec(memory_space=m) for m in (pltpu.VMEM, pl.ANY))
    return pl.pallas_call(
        conv_kernel,
        in_specs=[vmem] + [hbm] * 4,
        out_specs=vmem,
        out_shape=jax.ShapeDtypeStruct((blocks, chans, inner), BF16),
        scratch_shapes=[
            pltpu.VMEM((blocks, chans, inner), BF16),
            pltpu.VMEM(tile, BF16),
            pltpu.VMEM(tile, BF16),
            pltpu.VMEM(tile, F32),
        ]
        + [pltpu.VMEM(x.shape, x.dtype) for x in operands]
        + [pltpu.SemaphoreType.DMA((5,))],
        compiler_params=pltpu.CompilerParams(vmem_limit_bytes=24 << 20),
        cost_estimate=cost(6 * 10**9, 4 << 20),
        name="long_conv",
    )(gated, *operands)


PAD = 8


def short_sum(pad_ref, taps_ref, lane, rows):
    total = None
    for k in range(taps_ref.shape[0]):
        term = taps_ref[k : k + 1, pl.ds(lane, LANES)] * pad_ref[pl.ds(PAD - k, rows), :]
        total = term if total is None else total + term
    return total


def in_hbm(x):
    return pltpu.with_memory_space_constraint(x, pltpu.HBM)


PIECES = 4


def take_kernel(
    sig_any, key_any, query_any, taps_any, rim_ref, held_ref, wide_ref, query_ref, taps_ref, sems,
    tap_sem
):
    size = held_ref.shape[1] // PIECES
    streams = (
        (sig_any, held_ref.at[0]),
        (key_any, held_ref.at[1]),
        (query_any, query_ref),
    )
    copies = [
        [
            pltpu.make_async_copy(
                src.at[pl.ds(p * size, size), :], dst.at[pl.ds(p * size, size), :], sems.at[i, p]
            )
            for p in range(PIECES)
        ]
        for i, (src, dst) in enumerate(streams)
    ]
    tap_copy = pltpu.make_async_copy(taps_any, taps_ref, tap_sem)
    for stream in copies:
        for copy in stream:
            copy.start()
    tap_copy.start()
    for i, (stream, (_, held)) in enumerate(zip(copies, streams)):
        for p, copy in enumerate(stream):
            copy.wait()
            for lane in range(p * size, (p + 1) * size, LANES):
                turned = held[pl.ds(lane, LANES), :].T
                rim_ref[pl.ds(i * PAD, PAD), pl.ds(lane, LANES)] = turned[-PAD:]
    tap_copy.wait()
    wide_ref[...] = taps_ref[...].astype(F32)


def gate_kernel(held_ref, taps_ref, out_ref, head_ref, pad_ref):
    rows, chans = out_ref.shape[1:]
    pad_ref[:, :PAD] = jnp.zeros((2, PAD, LANES), F32)
    for lane in range(0, held_ref.shape[1], LANES):
        feats = []
        for i in range(2):
            turned = held_ref[i, pl.ds(lane, LANES), :].T.astype(F32)
            pad_ref[i, pl.ds(PAD, rows), :] = turned
            head_ref[i, :, pl.ds(lane, LANES)] = turned[:ROWS]
            feats.append(short_sum(pad_ref.at[i], taps_ref.at[i], lane, rows))
        out_ref[lane // chans, :, pl.ds(lane % chans, LANES)] = (feats[1] * feats[0]).astype(BF16)


def rim_kernel(head_ref, rim_ref, taps_ref, whole_ref, out_ref, pad_ref):
    blocks, rows, chans = out_ref.shape
    for lane in range(0, blocks * chans, LANES):
        feats = []
        for i in range(2):
            pad_ref[i, :PAD] = rim_ref[pl.ds(i * PAD, PAD), pl.ds(lane, LANES)].astype(F32)
            pad_ref[i, PAD:] = head_ref[i, :, pl.ds(lane, LANES)]
            feats.append(short_sum(pad_ref.at[i], taps_ref.at[i], lane, rows))
        out_ref[lane // chans, :, pl.ds(lane % chans, LANES)] = (feats[1] * feats[0]).astype(BF16)


def query_kernel(query_ref, rim_ref, taps_ref, out_ref, pad_ref):
    rows = query_ref.shape[1]
    for lane in range(0, query_ref.shape[0], LANES):
        pad_ref[:PAD] = rim_ref[:, pl.ds(lane, LANES)].astype(F32)
        pad_ref[PAD:] = query_ref[pl.ds(lane, LANES), :].T.astype(F32)
        out_ref[pl.ds(lane, LANES), :] = short_sum(pad_ref, taps_ref.at[2], lane, rows).T


def mix_kernel(conv_ref, query_ref, out_ref):
    for b in range(conv_ref.shape[0]):
        out_ref[b] = (conv_ref[b].astype(F32) * query_ref[b]).astype(BF16)


def fast_path(signal, input_gate, output_gate, short_taps, long_filter, bypass_gain):
    channels, rows = signal.shape
    tap_count = short_taps.shape[2]
    chans, length = long_filter.shape
    blocks = length // rows
    taps = short_taps.transpose(0, 2, 1)
    params = pltpu.CompilerParams(vmem_limit_bytes=VMEM_LIMIT)
    some = blocks // 4

    def stream_spec(count):
        return pl.BlockSpec((count * chans, rows), lambda i: (i, 0))

    def block_spec(count):
        return pl.BlockSpec((count, rows, chans), lambda i: (i, 0, 0))

    def taps_spec(count):
        return pl.BlockSpec((3, tap_count, count * chans), lambda i: (0, 0, i))

    vmem, hbm = (pl.BlockSpec(memory_space=m) for m in (pltpu.VMEM, pl.ANY))
    last, held, wide = pl.pallas_call(
        take_kernel,
        in_specs=[hbm] * 4,
        out_specs=[vmem] * 3,
        out_shape=[
            jax.ShapeDtypeStruct((3 * PAD, channels), BF16),
            jax.ShapeDtypeStruct((2, channels, rows), BF16),
            jax.ShapeDtypeStruct(taps.shape, F32),
        ],
        scratch_shapes=[
            pltpu.VMEM((channels, rows), BF16),
            pltpu.VMEM(taps.shape, BF16),
            pltpu.SemaphoreType.DMA((3, PIECES)),
            pltpu.SemaphoreType.DMA,
        ],
        compiler_params=params,
        cost_estimate=cost(10**8, 4 << 20),
        name="take",
    )(*(in_hbm(x) for x in (signal, input_gate, output_gate, taps)))
    rim = shifted(last, "ctx", 1)
    gated, head = pl.pallas_call(
        gate_kernel,
        grid=(blocks // some,),
        in_specs=[
            pl.BlockSpec((2, some * chans, rows), lambda i: (0, i, 0)),
            taps_spec(some),
        ],
        out_specs=[block_spec(some), pl.BlockSpec((2, ROWS, some * chans), lambda i: (0, 0, i))],
        out_shape=[
            jax.ShapeDtypeStruct((blocks, rows, chans), BF16),
            jax.ShapeDtypeStruct((2, ROWS, channels), F32),
        ],
        scratch_shapes=[pltpu.VMEM((2, PAD + rows, LANES), F32)],
        compiler_params=params,
        cost_estimate=cost(10**9, 8 << 20),
        name="gate_main",
    )(held, wide)
    gated = pl.pallas_call(
        rim_kernel,
        grid=(1,),
        in_specs=[
            whole((2, ROWS, channels)),
            whole((3 * PAD, channels)),
            whole((3, tap_count, channels)),
            pl.BlockSpec(memory_space=pl.ANY),
        ],
        out_specs=whole((blocks, ROWS, chans)),
        out_shape=jax.ShapeDtypeStruct((blocks, rows, chans), BF16),
        scratch_shapes=[pltpu.VMEM((2, PAD + ROWS, LANES), F32)],
        input_output_aliases={3: 0},
        compiler_params=params,
        cost_estimate=cost(10**7, 1 << 20),
        name="gate_rim",
    )(head, rim, wide, gated)
    arrived = lax.all_to_all(gated, "ctx", 0, 0)

    tables = transform_tables(blocks, rows)
    gain = bypass_gain.reshape(chans, 1)
    spectrum = filter_spectrum(long_filter, gain, tables, blocks)
    query = pl.pallas_call(
        query_kernel,
        grid=(blocks // some,),
        in_specs=[
            stream_spec(some),
            pl.BlockSpec((PAD, some * chans), lambda i: (2, i)),
            taps_spec(some),
        ],
        out_specs=stream_spec(some),
        out_shape=jax.ShapeDtypeStruct((channels, rows), F32),
        scratch_shapes=[pltpu.VMEM((PAD + rows, LANES), F32)],
        compiler_params=params,
        cost_estimate=cost(10**9, 8 << 20),
        name="query_feat",
    )(output_gate, rim, wide)

    arrived, query = lax.optimization_barrier((arrived, query))
    query = query.reshape(blocks, chans, rows)
    returned = lax.all_to_all(long_conv(arrived, spectrum, tables), "ctx", 0, 0)
    mix_spec = pl.BlockSpec((blocks // 2, chans, rows), lambda i: (i, 0, 0))
    mixed = pl.pallas_call(
        mix_kernel,
        grid=(2,),
        in_specs=[mix_spec, mix_spec],
        out_specs=mix_spec,
        out_shape=jax.ShapeDtypeStruct((blocks, chans, rows), BF16),
        compiler_params=params,
        cost_estimate=cost(10**8, 4 << 20),
        name="mix",
    )(returned, query)
    return mixed.reshape(channels, rows)


def on_device(signal, input_gate, output_gate, short_taps, long_filter, bypass_gain):
    channels, rows = signal.shape
    chans, length = long_filter.shape
    blocks = length // rows
    fits = (
        rows == LANES
        and chans % LANES == 0
        and chans * blocks == channels
        and blocks * rows == length
        and blocks in (4, 8, 16)
        and short_taps.shape[2] <= PAD
    )
    path = fast_path if fits else general_path
    return path(signal, input_gate, output_gate, short_taps, long_filter, bypass_gain)


def solution(mesh):
    placed = (
        P(None, ("groups", "ctx")),
        P(None, ("groups", "ctx")),
        P(None, ("groups", "ctx")),
        P(),
        P("ctx", None),
        P("ctx"),
    )
    return jax.shard_map(
        on_device, mesh=mesh, in_specs=placed, out_specs=P(None, ("groups", "ctx")), check_vma=False
    )
```

```python
import functools
import math

import jax
import jax.numpy as jnp
import numpy as np
from jax import lax
from jax.experimental import pallas as pl
from jax.experimental.pallas import tpu as pltpu
from jax.sharding import PartitionSpec as P

F32, BF16 = jnp.float32, jnp.bfloat16
VMEM_LIMIT = 12 << 20
LANES = 128


def shifted(shard, axis, by):
    count = lax.axis_size(axis)
    pairs = [(i, i + by) for i in range(count) if 0 <= i + by < count]
    return lax.ppermute(shard, axis, pairs)


def short_conv(values, taps, rim):
    tap_count = taps.shape[1]
    length = values.shape[1]
    padded = jnp.concatenate([rim, values], axis=1)
    total = jnp.zeros_like(values)
    for k in range(tap_count):
        total = (
            total + taps[:, k : k + 1] * padded[:, tap_count - 1 - k : tap_count - 1 - k + length]
        )
    return total


def dft_tables(height, breadth, period):
    rindex = lax.broadcasted_iota(jnp.int32, (height, breadth), 0)
    cindex = lax.broadcasted_iota(jnp.int32, (height, breadth), 1)
    phase_angle = (rindex * cindex % period).astype(F32) * (2.0 * math.pi / period)
    return (jnp.cos(phase_angle), jnp.sin(phase_angle))


def split_table(table):
    upper = table.astype(BF16)
    lower = (table - upper.astype(F32)).astype(BF16)
    return (upper, lower)


def precise(pattern, left_op, right_op):
    return jnp.einsum(pattern, left_op, right_op, precision=lax.Precision.HIGHEST)


def narrow(pattern, parts, right_op):
    first = jnp.einsum(pattern, parts[0], right_op, preferred_element_type=F32)
    return first + jnp.einsum(pattern, parts[1], right_op, preferred_element_type=F32)


def make_tables(length):
    breadth = 128
    height = 2 * length // breadth
    row_tables = dft_tables(height, height // 2, height)
    twist_tables = dft_tables(height, breadth, 2 * length)
    col_tables = dft_tables(breadth, breadth, breadth)
    row_split = (split_table(row_tables[0]), split_table(row_tables[1]))
    return (row_tables, twist_tables, col_tables, row_split)


def forward_dft(values, tables):
    row_tables, twist_tables, col_tables, row_split = tables
    chan_count, length = values.shape
    folded = values.reshape(chan_count, length // 128, 128)
    first_re = narrow("kp,cpq->ckq", row_split[0], folded)
    first_im = -narrow("kp,cpq->ckq", row_split[1], folded)
    turned_re = first_re * twist_tables[0] + first_im * twist_tables[1]
    turned_im = first_im * twist_tables[0] - first_re * twist_tables[1]
    spec_re = precise("ckq,qm->ckm", turned_re, col_tables[0]) + precise(
        "ckq,qm->ckm", turned_im, col_tables[1]
    )
    spec_im = precise("ckq,qm->ckm", turned_im, col_tables[0]) - precise(
        "ckq,qm->ckm", turned_re, col_tables[1]
    )
    return (spec_re, spec_im)


def inverse_dft(spec_re, spec_im, tables, length):
    row_tables, twist_tables, col_tables, row_split = tables
    chan_count = spec_re.shape[0]
    back_re = precise("ckm,mq->ckq", spec_re, col_tables[0]) - precise(
        "ckm,mq->ckq", spec_im, col_tables[1]
    )
    back_im = precise("ckm,mq->ckq", spec_re, col_tables[1]) + precise(
        "ckm,mq->ckq", spec_im, col_tables[0]
    )
    twist_re = back_re * twist_tables[0] - back_im * twist_tables[1]
    twist_im = back_re * twist_tables[1] + back_im * twist_tables[0]
    folded = precise("kp,ckq->cpq", row_tables[0], twist_re) - precise(
        "kp,ckq->cpq", row_tables[1], twist_im
    )
    return (folded / (2.0 * length)).reshape(chan_count, length)


def long_mix(gated_narrow, kernel, bypass):
    length = gated_narrow.shape[1]
    tables = make_tables(length)
    kern_re, kern_im = forward_dft(kernel, tables)
    sig_re, sig_im = forward_dft(gated_narrow, tables)
    prod_re = sig_re * kern_re - sig_im * kern_im
    prod_im = sig_re * kern_im + sig_im * kern_re
    return inverse_dft(prod_re, prod_im, tables, length) + bypass[:, None] * gated_narrow.astype(
        F32
    )


def general_path(signal, input_gate, output_gate, short_taps, long_filter, bypass_gain):
    channels, local_tokens = signal.shape
    rim_len = short_taps.shape[2] - 1
    taps = short_taps.astype(F32)
    feats = []
    for i, stream in enumerate((signal, input_gate, output_gate)):
        rim = shifted(stream[:, local_tokens - rim_len :], "ctx", 1)
        feats.append(short_conv(stream.astype(F32), taps[i], rim.astype(F32)))
    gated = (feats[1] * feats[0]).astype(BF16)
    gated = lax.all_to_all(gated, "ctx", split_axis=0, concat_axis=1, tiled=True)
    longconv = long_mix(gated, long_filter, bypass_gain).astype(BF16)
    returned = lax.all_to_all(longconv, "ctx", split_axis=1, concat_axis=0, tiled=True)
    return (feats[2] * returned.astype(F32)).astype(BF16)


def add(a, b):
    return b if a is None else a if b is None else a + b


def sub(a, b):
    return a if b is None else -b if a is None else a - b


def turn(value, k, n):
    re, im = value
    k %= n
    if k == 0:
        return value
    if 4 * k == n:
        return (None if im is None else -im, re)
    if 4 * k == 3 * n:
        return (im, None if re is None else -re)
    c, s = math.cos(2 * math.pi * k / n), math.sin(2 * math.pi * k / n)
    if im is None:
        return (re * c, re * s)
    if re is None:
        return (im * -s, im * c)
    return (re * c - im * s, re * s + im * c)


def rfft(xs):
    n = len(xs)
    if n == 1:
        return [(xs[0], None)]
    half = n // 2
    even, odd = rfft(xs[0::2]), rfft(xs[1::2])
    out = [None] * (half + 1)
    for k in range(half // 2 + 1):
        e, t = even[k], turn(odd[k], -k, n)
        out[k] = (add(e[0], t[0]), add(e[1], t[1]))
        if half - k != k:
            out[half - k] = (sub(e[0], t[0]), sub(t[1], e[1]))
    return out


def irfft_first_half(zs):
    half = len(zs) - 1
    n = 2 * half
    if n == 2:
        return [add(zs[0][0], zs[1][0])]
    even, odd = [], []
    for k in range(half // 2 + 1):
        a, b = zs[k], zs[half - k]
        if k == half - k:
            even.append((a[0] * 2.0, None))
            odd.append((a[1] * -2.0, None))
            continue
        even.append((add(a[0], b[0]), sub(a[1], b[1])))
        odd.append(turn((sub(a[0], b[0]), add(a[1], b[1])), k, n))
    first, second = irfft_first_half(even), irfft_first_half(odd)
    return [v for pair in zip(first, second) for v in pair]


def hi_lo(value):
    upper = value.astype(BF16)
    return upper, (value - upper.astype(F32)).astype(BF16)


def np_hi_lo(table):
    table = table.astype(np.float32)
    upper = table.astype(jnp.bfloat16)
    return [upper, (table - upper.astype(np.float32)).astype(jnp.bfloat16)]


def transform_tables(blocks, inner):
    index = np.arange(inner)
    angle = 2 * np.pi * (np.outer(index, index) % inner) / inner
    c, s = np.cos(angle), np.sin(angle)
    turns = np.pi * np.outer(np.arange(blocks + 1), index) / (blocks * inner)
    forward, backward = (
        jnp.asarray(np.concatenate([upper, upper, lower]))
        for upper, lower in (
            np_hi_lo(np.block([[c, -s], [s, c]])),
            np_hi_lo(np.block([[c, s], [-s, c]]) / (2 * blocks * inner)),
        )
    )
    return forward, backward, jnp.asarray(np.stack([np.cos(turns), np.sin(turns)]), F32)


ROWS = 16


def over_rows(rows, body):
    def step(t, carry):
        body(pl.multiple_of(t * ROWS, ROWS))
        return carry

    lax.fori_loop(0, rows // ROWS, step, 0, unroll=2)


def outer_forward(load, blocks, turn_ref, hi_ref, lo_ref):
    freqs, chans, width = hi_ref.shape
    inner = width // 2

    def tile(row):
        xs = [load(b, row).astype(F32) for b in range(blocks)]
        for k, (re, im) in enumerate(rfft(xs + [None] * blocks)):
            if k:
                c, s = turn_ref[0, k : k + 1, :], turn_ref[1, k : k + 1, :]
                if im is None:
                    re, im = re * c, -(re * s)
                else:
                    re, im = re * c + im * s, im * c - re * s
            if im is None:
                im = jnp.zeros_like(re)
            for part, base in ((re, 0), (im, inner)):
                upper, lower = hi_lo(part)
                hi_ref[k, pl.ds(row, ROWS), pl.ds(base, inner)] = upper
                lo_ref[k, pl.ds(row, ROWS), pl.ds(base, inner)] = lower

    over_rows(chans, tile)


def inner_product(upper, lower, table_ref):
    stacked = jnp.concatenate([upper, lower, upper], axis=1)
    return jnp.dot(stacked, table_ref[...], preferred_element_type=F32)


def groups_of(count, size):
    return [range(k, min(k + size, count)) for k in range(0, count, size)]


STACK = 2
TILE = 16


def stacked_rows(ref, ks):
    return ref[ks[0] : ks[-1] + 1].reshape(len(ks) * ref.shape[1], ref.shape[2])


def spectrum_kernel(filt_ref, gain_ref, turn_ref, fwd_ref, spec_ref, hi_ref, lo_ref):
    chans = filt_ref.shape[0]
    inner = hi_ref.shape[2] // 2
    blocks = hi_ref.shape[0] - 1
    outer_forward(
        lambda b, row: filt_ref[pl.ds(row, ROWS), b * inner : (b + 1) * inner],
        blocks,
        turn_ref,
        hi_ref,
        lo_ref,
    )
    gain = gain_ref[...]
    for ks in groups_of(blocks + 1, STACK):
        spec = inner_product(stacked_rows(hi_ref, ks), stacked_rows(lo_ref, ks), fwd_ref)
        for i, k in enumerate(ks):
            part = spec[i * chans : (i + 1) * chans]
            spec_ref[k, :, :inner] = part[:, :inner] + gain
            spec_ref[k, :, inner:] = part[:, inner:]


def conv_kernel(
    gated_ref, spec_any, turn_any, fwd_any, bwd_any, out_any, turned_ref, hi_ref, lo_ref, back_ref,
    out_ref, spec_ref, turn_ref, fwd_ref, bwd_ref, sems, out_sems
):
    blocks, inner, chans = gated_ref.shape
    freqs = blocks + 1
    tiles = chans // TILE
    copies = [
        pltpu.make_async_copy(src, dst, sems.at[i])
        for i, (src, dst) in enumerate(
            (
                (turn_any, turn_ref),
                (fwd_any, fwd_ref),
                (bwd_any, bwd_ref),
                (spec_any.at[:, : chans // 2], spec_ref.at[:, : chans // 2]),
                (spec_any.at[:, chans // 2 :], spec_ref.at[:, chans // 2 :]),
            )
        )
    ]
    for copy in copies:
        copy.start()
    for b in range(blocks):
        turned_ref[b] = gated_ref[b].T
    copies[0].wait()

    def outer(t):
        def tile(row):
            xs = [turned_ref[b, t * TILE + row : t * TILE + row + ROWS].astype(F32) for b in range(blocks)]
            for k, (re, im) in enumerate(rfft(xs + [None] * blocks)):
                if k:
                    c, s = turn_ref[0, k : k + 1, :], turn_ref[1, k : k + 1, :]
                    if im is None:
                        re, im = re * c, -(re * s)
                    else:
                        re, im = re * c + im * s, im * c - re * s
                if im is None:
                    im = jnp.zeros_like(re)
                for part, base in ((re, 0), (im, inner)):
                    upper, lower = hi_lo(part)
                    hi_ref[t % 2, k, row : row + ROWS, base : base + inner] = upper
                    lo_ref[t % 2, k, row : row + ROWS, base : base + inner] = lower

        for row in range(0, TILE, ROWS):
            tile(row)

    def flat(x):
        return x.reshape(freqs * TILE, 2 * inner)

    def inverse(t):
        for row in range(0, TILE, ROWS):
            zs = []
            for k in range(freqs):
                re = back_ref[t % 2, k, row : row + ROWS, :inner]
                if k == 0:
                    zs.append((re, None))
                    continue
                im = back_ref[t % 2, k, row : row + ROWS, inner:]
                c, s = turn_ref[0, k : k + 1, :], turn_ref[1, k : k + 1, :]
                zs.append((re * c - im * s, None if k == blocks else re * s + im * c))
            for b, value in enumerate(irfft_first_half(zs)):
                out_ref[b, t * TILE + row : t * TILE + row + ROWS, :] = value.astype(BF16)
        part, last = t // group, (t + 1) % group == 0
        if last:
            here = pl.ds(part * group * TILE, group * TILE)
            sent.append(
                pltpu.make_async_copy(out_ref.at[:, here], out_any.at[:, here], out_sems.at[part])
            )
            sent[-1].start()

    sent, group = [], tiles // out_sems.shape[0]
    outer(0)
    copies[1].wait()
    copies[2].wait()
    for t in range(tiles):
        if t in (0, tiles // 2):
            copies[3 if t == 0 else 4].wait()
        sig = inner_product(flat(hi_ref[t % 2]), flat(lo_ref[t % 2]), fwd_ref)
        if t + 1 < tiles:
            outer(t + 1)
        ker = flat(spec_ref[:, t * TILE : (t + 1) * TILE])
        sig_re, sig_im, ker_re, ker_im = (
            x[:, at : at + inner] for x in (sig, ker) for at in (0, inner)
        )
        prod = jnp.concatenate(
            [sig_re * ker_re - sig_im * ker_im, sig_re * ker_im + sig_im * ker_re], axis=1
        )
        back = inner_product(*hi_lo(prod), bwd_ref)
        back_ref[t % 2] = back.reshape(freqs, TILE, 2 * inner)
        if t:
            inverse(t - 1)
    inverse(tiles - 1)
    for copy in sent:
        copy.wait()


def cost(flops, size):
    return pl.CostEstimate(flops=flops, bytes_accessed=size, transcendentals=0)


def whole(shape):
    return pl.BlockSpec(shape, lambda i: (0,) * len(shape))


def filter_spectrum(filt, gain, tables, blocks):
    forward, _, turns = tables
    chans, inner = filt.shape[0], filt.shape[1] // blocks
    shape = (blocks + 1, chans, 2 * inner)
    return pl.pallas_call(
        spectrum_kernel,
        out_shape=jax.ShapeDtypeStruct(shape, F32),
        scratch_shapes=[pltpu.VMEM(shape, BF16)] * 2,
        compiler_params=pltpu.CompilerParams(vmem_limit_bytes=20 << 20),
        cost_estimate=cost(3 * 10**9, 4 << 20),
        name="filter_spectrum",
    )(filt, gain, turns, forward)


def long_conv(gated, spectrum, tables):
    forward, backward, turns = tables
    blocks, inner, chans = gated.shape
    tile = (2, blocks + 1, TILE, 2 * inner)
    operands = [in_hbm(x) for x in (spectrum, turns, forward, backward)]
    vmem, hbm = (pl.BlockSpec(memory_space=m) for m in (pltpu.VMEM, pl.ANY))
    return pl.pallas_call(
        conv_kernel,
        in_specs=[vmem] + [hbm] * 4,
        out_specs=hbm,
        out_shape=jax.ShapeDtypeStruct((blocks, chans, inner), BF16),
        scratch_shapes=[
            pltpu.VMEM((blocks, chans, inner), BF16),
            pltpu.VMEM(tile, BF16),
            pltpu.VMEM(tile, BF16),
            pltpu.VMEM(tile, F32),
            pltpu.VMEM((blocks, chans, inner), BF16),
        ]
        + [pltpu.VMEM(x.shape, x.dtype) for x in operands]
        + [pltpu.SemaphoreType.DMA((5,)), pltpu.SemaphoreType.DMA((8,))],
        compiler_params=pltpu.CompilerParams(vmem_limit_bytes=24 << 20),
        cost_estimate=cost(6 * 10**9, 4 << 20),
        name="long_conv",
    )(gated, *operands)


PAD = 8


def short_sum(pad_ref, taps_ref, lane, rows):
    total = None
    for k in range(taps_ref.shape[0]):
        term = taps_ref[k : k + 1, pl.ds(lane, LANES)] * pad_ref[pl.ds(PAD - k, rows), :]
        total = term if total is None else total + term
    return total


def in_hbm(x):
    return pltpu.with_memory_space_constraint(x, pltpu.HBM)


PIECES = 2


def tail_kernel(stream_ref, out_ref):
    for lane in range(0, stream_ref.shape[0], LANES):
        out_ref[:, pl.ds(lane, LANES)] = stream_ref[pl.ds(lane, LANES), :].T[-PAD:]


def take_kernel(sig_any, key_any, taps_any, rim_ref, held_ref, wide_ref, taps_ref, sems, tap_sem):
    size = held_ref.shape[1] // PIECES
    copies = [
        [
            pltpu.make_async_copy(
                src.at[pl.ds(p * size, size), :],
                held_ref.at[i, pl.ds(p * size, size), :],
                sems.at[i, p],
            )
            for p in range(PIECES)
        ]
        for i, src in enumerate((sig_any, key_any))
    ]
    tap_copy = pltpu.make_async_copy(taps_any, taps_ref, tap_sem)
    for stream in copies:
        for copy in stream:
            copy.start()
    tap_copy.start()
    for i, stream in enumerate(copies):
        for p, copy in enumerate(stream):
            copy.wait()
            for lane in range(p * size, (p + 1) * size, LANES):
                turned = held_ref[i, pl.ds(lane, LANES), :].T
                rim_ref[pl.ds(i * PAD, PAD), pl.ds(lane, LANES)] = turned[-PAD:]
    tap_copy.wait()
    wide_ref[...] = taps_ref[...].astype(F32)


def send_off(part, size, src_ref, dst_any, sems):
    copy = pltpu.make_async_copy(
        src_ref.at[part * size : (part + 1) * size],
        dst_any.at[part * size : (part + 1) * size],
        sems.at[part],
    )
    copy.start()
    return copy


def gate_kernel(held_ref, taps_ref, out_any, head_ref, pad_ref, block_ref, sems):
    blocks, rows, chans = block_ref.shape
    size = blocks // sems.shape[0]
    pad_ref[:, :PAD] = jnp.zeros((2, PAD, LANES), F32)
    copies = []
    for part in range(sems.shape[0]):
        for lane in range(part * size * chans, (part + 1) * size * chans, LANES):
            feats = []
            for i in range(2):
                turned = held_ref[i, pl.ds(lane, LANES), :].T.astype(F32)
                pad_ref[i, pl.ds(PAD, rows), :] = turned
                head_ref[i, :, pl.ds(lane, LANES)] = turned[:ROWS]
                feats.append(short_sum(pad_ref.at[i], taps_ref.at[i], lane, rows))
            block_ref[lane // chans, :, pl.ds(lane % chans, LANES)] = (
                feats[1] * feats[0]
            ).astype(BF16)
        copies.append(send_off(part, size, block_ref, out_any, sems))
    for copy in copies:
        copy.wait()


def rim_kernel(
    head_ref, rim_ref, taps_ref, whole_any, out_any, pad_ref, block_ref, sem
):
    blocks, rows, chans = block_ref.shape
    for lane in range(0, blocks * chans, LANES):
        feats = []
        for i in range(2):
            pad_ref[i, :PAD] = rim_ref[pl.ds(i * PAD, PAD), pl.ds(lane, LANES)].astype(F32)
            pad_ref[i, PAD:] = head_ref[i, :, pl.ds(lane, LANES)]
            feats.append(short_sum(pad_ref.at[i], taps_ref.at[i], lane, rows))
        block_ref[lane // chans, :, pl.ds(lane % chans, LANES)] = (feats[1] * feats[0]).astype(BF16)
    copy = pltpu.make_async_copy(block_ref, out_any.at[:, :rows], sem)
    copy.start()
    copy.wait()


def query_kernel(query_ref, rim_ref, taps_ref, out_ref, pad_ref):
    rows = query_ref.shape[1]
    for lane in range(0, query_ref.shape[0], LANES):
        pad_ref[:PAD] = rim_ref[:, pl.ds(lane, LANES)].astype(F32)
        pad_ref[PAD:] = query_ref[pl.ds(lane, LANES), :].T.astype(F32)
        out_ref[pl.ds(lane, LANES), :] = short_sum(pad_ref, taps_ref.at[2], lane, rows).T


def mix_kernel(conv_ref, query_ref, out_any, block_ref, sems):
    size = block_ref.shape[0] // sems.shape[0]
    copies = []
    for part in range(sems.shape[0]):
        for b in range(part * size, (part + 1) * size):
            block_ref[b] = (conv_ref[b].astype(F32) * query_ref[b]).astype(BF16)
        copies.append(send_off(part, size, block_ref, out_any, sems))
    for copy in copies:
        copy.wait()


def fast_path(signal, input_gate, output_gate, short_taps, long_filter, bypass_gain):
    channels, rows = signal.shape
    tap_count = short_taps.shape[2]
    chans, length = long_filter.shape
    blocks = length // rows
    taps = short_taps.transpose(0, 2, 1)
    params = pltpu.CompilerParams(vmem_limit_bytes=VMEM_LIMIT)
    some = blocks // 4

    def stream_spec(count):
        return pl.BlockSpec((count * chans, rows), lambda i: (i, 0))

    def block_spec(count):
        return pl.BlockSpec((count, rows, chans), lambda i: (i, 0, 0))

    def taps_spec(count):
        return pl.BlockSpec((3, tap_count, count * chans), lambda i: (0, 0, i))

    vmem, hbm = (pl.BlockSpec(memory_space=m) for m in (pltpu.VMEM, pl.ANY))
    last, held, wide = pl.pallas_call(
        take_kernel,
        in_specs=[hbm] * 3,
        out_specs=[vmem] * 3,
        out_shape=[
            jax.ShapeDtypeStruct((2 * PAD, channels), BF16),
            jax.ShapeDtypeStruct((2, channels, rows), BF16),
            jax.ShapeDtypeStruct(taps.shape, F32),
        ],
        scratch_shapes=[
            pltpu.VMEM(taps.shape, BF16),
            pltpu.SemaphoreType.DMA((2, PIECES)),
            pltpu.SemaphoreType.DMA,
        ],
        compiler_params=params,
        cost_estimate=cost(10**8, 4 << 20),
        name="take",
    )(*(in_hbm(x) for x in (signal, input_gate, taps)))
    rim = shifted(last, "ctx", 1)
    parts = blocks // 2
    gated, head = pl.pallas_call(
        gate_kernel,
        in_specs=[vmem] * 2,
        out_specs=[hbm, vmem],
        out_shape=[
            jax.ShapeDtypeStruct((blocks, rows, chans), BF16),
            jax.ShapeDtypeStruct((2, ROWS, channels), F32),
        ],
        scratch_shapes=[
            pltpu.VMEM((2, PAD + rows, LANES), F32),
            pltpu.VMEM((blocks, rows, chans), BF16),
            pltpu.SemaphoreType.DMA((parts,)),
        ],
        compiler_params=params,
        cost_estimate=cost(10**9, 8 << 20),
        name="gate_main",
    )(held, wide)
    gated = pl.pallas_call(
        rim_kernel,
        in_specs=[vmem] * 3 + [hbm],
        out_specs=hbm,
        out_shape=jax.ShapeDtypeStruct((blocks, rows, chans), BF16),
        scratch_shapes=[
            pltpu.VMEM((2, PAD + ROWS, LANES), F32),
            pltpu.VMEM((blocks, ROWS, chans), BF16),
            pltpu.SemaphoreType.DMA,
        ],
        input_output_aliases={3: 0},
        compiler_params=params,
        cost_estimate=cost(10**7, 1 << 20),
        name="gate_rim",
    )(head, rim, wide, gated)
    arrived = lax.all_to_all(gated, "ctx", 0, 0)

    tables = transform_tables(blocks, rows)
    gain = bypass_gain.reshape(chans, 1)
    spectrum = filter_spectrum(long_filter, gain, tables, blocks)
    query_last = pl.pallas_call(
        tail_kernel,
        out_shape=jax.ShapeDtypeStruct((PAD, channels), BF16),
        compiler_params=params,
        cost_estimate=cost(10**8, 2 << 20),
        name="query_last",
    )(output_gate)
    query_rim = shifted(query_last, "ctx", 1)
    arrived, query_rim = lax.optimization_barrier((arrived, query_rim))
    query = pl.pallas_call(
        query_kernel,
        grid=(blocks // some,),
        in_specs=[
            stream_spec(some),
            pl.BlockSpec((PAD, some * chans), lambda i: (0, i)),
            taps_spec(some),
        ],
        out_specs=stream_spec(some),
        out_shape=jax.ShapeDtypeStruct((channels, rows), F32),
        scratch_shapes=[pltpu.VMEM((PAD + rows, LANES), F32)],
        compiler_params=params,
        cost_estimate=cost(10**9, 8 << 20),
        name="query_feat",
    )(output_gate, query_rim, wide)

    query = query.reshape(blocks, chans, rows)
    returned = lax.all_to_all(long_conv(arrived, spectrum, tables), "ctx", 0, 0)
    mixed = pl.pallas_call(
        mix_kernel,
        in_specs=[vmem] * 2,
        out_specs=hbm,
        out_shape=jax.ShapeDtypeStruct((blocks, chans, rows), BF16),
        scratch_shapes=[
            pltpu.VMEM((blocks, chans, rows), BF16),
            pltpu.SemaphoreType.DMA((parts,)),
        ],
        compiler_params=params,
        cost_estimate=cost(10**8, 4 << 20),
        name="mix",
    )(returned, query)
    return mixed.reshape(channels, rows)


def on_device(signal, input_gate, output_gate, short_taps, long_filter, bypass_gain):
    channels, rows = signal.shape
    chans, length = long_filter.shape
    blocks = length // rows
    fits = (
        rows == LANES
        and chans % LANES == 0
        and chans * blocks == channels
        and blocks * rows == length
        and blocks in (4, 8, 16)
        and short_taps.shape[2] <= PAD
    )
    path = fast_path if fits else general_path
    return path(signal, input_gate, output_gate, short_taps, long_filter, bypass_gain)


def solution(mesh):
    placed = (
        P(None, ("groups", "ctx")),
        P(None, ("groups", "ctx")),
        P(None, ("groups", "ctx")),
        P(),
        P("ctx", None),
        P("ctx"),
    )
    return jax.shard_map(
        on_device, mesh=mesh, in_specs=placed, out_specs=P(None, ("groups", "ctx")), check_vma=False
    )
```

```python
import functools
import math

import jax
import jax.numpy as jnp
import numpy as np
from jax import lax
from jax.experimental import pallas as pl
from jax.experimental.pallas import tpu as pltpu
from jax.sharding import PartitionSpec as P

F32, BF16 = jnp.float32, jnp.bfloat16
VMEM_LIMIT = 12 << 20
LANES = 128


def shifted(shard, axis, by):
    count = lax.axis_size(axis)
    pairs = [(i, i + by) for i in range(count) if 0 <= i + by < count]
    return lax.ppermute(shard, axis, pairs)


def short_conv(values, taps, rim):
    tap_count = taps.shape[1]
    length = values.shape[1]
    padded = jnp.concatenate([rim, values], axis=1)
    total = jnp.zeros_like(values)
    for k in range(tap_count):
        total = (
            total + taps[:, k : k + 1] * padded[:, tap_count - 1 - k : tap_count - 1 - k + length]
        )
    return total


def dft_tables(height, breadth, period):
    rindex = lax.broadcasted_iota(jnp.int32, (height, breadth), 0)
    cindex = lax.broadcasted_iota(jnp.int32, (height, breadth), 1)
    phase_angle = (rindex * cindex % period).astype(F32) * (2.0 * math.pi / period)
    return (jnp.cos(phase_angle), jnp.sin(phase_angle))


def split_table(table):
    upper = table.astype(BF16)
    lower = (table - upper.astype(F32)).astype(BF16)
    return (upper, lower)


def precise(pattern, left_op, right_op):
    return jnp.einsum(pattern, left_op, right_op, precision=lax.Precision.HIGHEST)


def narrow(pattern, parts, right_op):
    first = jnp.einsum(pattern, parts[0], right_op, preferred_element_type=F32)
    return first + jnp.einsum(pattern, parts[1], right_op, preferred_element_type=F32)


def make_tables(length):
    breadth = 128
    height = 2 * length // breadth
    row_tables = dft_tables(height, height // 2, height)
    twist_tables = dft_tables(height, breadth, 2 * length)
    col_tables = dft_tables(breadth, breadth, breadth)
    row_split = (split_table(row_tables[0]), split_table(row_tables[1]))
    return (row_tables, twist_tables, col_tables, row_split)


def forward_dft(values, tables):
    row_tables, twist_tables, col_tables, row_split = tables
    chan_count, length = values.shape
    folded = values.reshape(chan_count, length // 128, 128)
    first_re = narrow("kp,cpq->ckq", row_split[0], folded)
    first_im = -narrow("kp,cpq->ckq", row_split[1], folded)
    turned_re = first_re * twist_tables[0] + first_im * twist_tables[1]
    turned_im = first_im * twist_tables[0] - first_re * twist_tables[1]
    spec_re = precise("ckq,qm->ckm", turned_re, col_tables[0]) + precise(
        "ckq,qm->ckm", turned_im, col_tables[1]
    )
    spec_im = precise("ckq,qm->ckm", turned_im, col_tables[0]) - precise(
        "ckq,qm->ckm", turned_re, col_tables[1]
    )
    return (spec_re, spec_im)


def inverse_dft(spec_re, spec_im, tables, length):
    row_tables, twist_tables, col_tables, row_split = tables
    chan_count = spec_re.shape[0]
    back_re = precise("ckm,mq->ckq", spec_re, col_tables[0]) - precise(
        "ckm,mq->ckq", spec_im, col_tables[1]
    )
    back_im = precise("ckm,mq->ckq", spec_re, col_tables[1]) + precise(
        "ckm,mq->ckq", spec_im, col_tables[0]
    )
    twist_re = back_re * twist_tables[0] - back_im * twist_tables[1]
    twist_im = back_re * twist_tables[1] + back_im * twist_tables[0]
    folded = precise("kp,ckq->cpq", row_tables[0], twist_re) - precise(
        "kp,ckq->cpq", row_tables[1], twist_im
    )
    return (folded / (2.0 * length)).reshape(chan_count, length)


def long_mix(gated_narrow, kernel, bypass):
    length = gated_narrow.shape[1]
    tables = make_tables(length)
    kern_re, kern_im = forward_dft(kernel, tables)
    sig_re, sig_im = forward_dft(gated_narrow, tables)
    prod_re = sig_re * kern_re - sig_im * kern_im
    prod_im = sig_re * kern_im + sig_im * kern_re
    return inverse_dft(prod_re, prod_im, tables, length) + bypass[:, None] * gated_narrow.astype(
        F32
    )


def general_path(signal, input_gate, output_gate, short_taps, long_filter, bypass_gain):
    channels, local_tokens = signal.shape
    rim_len = short_taps.shape[2] - 1
    taps = short_taps.astype(F32)
    feats = []
    for i, stream in enumerate((signal, input_gate, output_gate)):
        rim = shifted(stream[:, local_tokens - rim_len :], "ctx", 1)
        feats.append(short_conv(stream.astype(F32), taps[i], rim.astype(F32)))
    gated = (feats[1] * feats[0]).astype(BF16)
    gated = lax.all_to_all(gated, "ctx", split_axis=0, concat_axis=1, tiled=True)
    longconv = long_mix(gated, long_filter, bypass_gain).astype(BF16)
    returned = lax.all_to_all(longconv, "ctx", split_axis=1, concat_axis=0, tiled=True)
    return (feats[2] * returned.astype(F32)).astype(BF16)


def add(a, b):
    return b if a is None else a if b is None else a + b


def sub(a, b):
    return a if b is None else -b if a is None else a - b


def turn(value, k, n):
    re, im = value
    k %= n
    if k == 0:
        return value
    if 4 * k == n:
        return (None if im is None else -im, re)
    if 4 * k == 3 * n:
        return (im, None if re is None else -re)
    c, s = math.cos(2 * math.pi * k / n), math.sin(2 * math.pi * k / n)
    if im is None:
        return (re * c, re * s)
    if re is None:
        return (im * -s, im * c)
    return (re * c - im * s, re * s + im * c)


def rfft(xs):
    n = len(xs)
    if n == 1:
        return [(xs[0], None)]
    half = n // 2
    even, odd = rfft(xs[0::2]), rfft(xs[1::2])
    out = [None] * (half + 1)
    for k in range(half // 2 + 1):
        e, t = even[k], turn(odd[k], -k, n)
        out[k] = (add(e[0], t[0]), add(e[1], t[1]))
        if half - k != k:
            out[half - k] = (sub(e[0], t[0]), sub(t[1], e[1]))
    return out


def irfft_first_half(zs):
    half = len(zs) - 1
    n = 2 * half
    if n == 2:
        return [add(zs[0][0], zs[1][0])]
    even, odd = [], []
    for k in range(half // 2 + 1):
        a, b = zs[k], zs[half - k]
        if k == half - k:
            even.append((a[0] * 2.0, None))
            odd.append((a[1] * -2.0, None))
            continue
        even.append((add(a[0], b[0]), sub(a[1], b[1])))
        odd.append(turn((sub(a[0], b[0]), add(a[1], b[1])), k, n))
    first, second = irfft_first_half(even), irfft_first_half(odd)
    return [v for pair in zip(first, second) for v in pair]


def hi_lo(value):
    upper = value.astype(BF16)
    return upper, (value - upper.astype(F32)).astype(BF16)


def np_hi_lo(table):
    table = table.astype(np.float32)
    upper = table.astype(jnp.bfloat16)
    return [upper, (table - upper.astype(np.float32)).astype(jnp.bfloat16)]


def transform_tables(blocks, inner):
    index = np.arange(inner)
    angle = 2 * np.pi * (np.outer(index, index) % inner) / inner
    c, s = np.cos(angle), np.sin(angle)
    turns = np.pi * np.outer(np.arange(blocks + 1), index) / (blocks * inner)
    forward, backward = (
        jnp.asarray(np.concatenate([upper, upper, lower]))
        for upper, lower in (
            np_hi_lo(np.block([[c, -s], [s, c]])),
            np_hi_lo(np.block([[c, s], [-s, c]]) / (2 * blocks * inner)),
        )
    )
    return forward, backward, jnp.asarray(np.stack([np.cos(turns), np.sin(turns)]), F32)


ROWS = 16


def over_rows(rows, body):
    def step(t, carry):
        body(pl.multiple_of(t * ROWS, ROWS))
        return carry

    lax.fori_loop(0, rows // ROWS, step, 0, unroll=2)


def outer_forward(load, blocks, turn_ref, hi_ref, lo_ref):
    freqs, chans, width = hi_ref.shape
    inner = width // 2

    def tile(row):
        xs = [load(b, row).astype(F32) for b in range(blocks)]
        for k, (re, im) in enumerate(rfft(xs + [None] * blocks)):
            if k:
                c, s = turn_ref[0, k : k + 1, :], turn_ref[1, k : k + 1, :]
                if im is None:
                    re, im = re * c, -(re * s)
                else:
                    re, im = re * c + im * s, im * c - re * s
            if im is None:
                im = jnp.zeros_like(re)
            for part, base in ((re, 0), (im, inner)):
                upper, lower = hi_lo(part)
                hi_ref[k, pl.ds(row, ROWS), pl.ds(base, inner)] = upper
                lo_ref[k, pl.ds(row, ROWS), pl.ds(base, inner)] = lower

    over_rows(chans, tile)


def inner_product(upper, lower, table_ref):
    stacked = jnp.concatenate([upper, lower, upper], axis=1)
    return jnp.dot(stacked, table_ref[...], preferred_element_type=F32)


def groups_of(count, size):
    return [range(k, min(k + size, count)) for k in range(0, count, size)]


STACK = 2
TILE = 16


def stacked_rows(ref, ks):
    return ref[ks[0] : ks[-1] + 1].reshape(len(ks) * ref.shape[1], ref.shape[2])


def spectrum_kernel(filt_ref, gain_ref, turn_ref, fwd_ref, spec_ref, hi_ref, lo_ref):
    chans = filt_ref.shape[0]
    inner = hi_ref.shape[2] // 2
    blocks = hi_ref.shape[0] - 1
    outer_forward(
        lambda b, row: filt_ref[pl.ds(row, ROWS), b * inner : (b + 1) * inner],
        blocks,
        turn_ref,
        hi_ref,
        lo_ref,
    )
    gain = gain_ref[...]
    for ks in groups_of(blocks + 1, STACK):
        spec = inner_product(stacked_rows(hi_ref, ks), stacked_rows(lo_ref, ks), fwd_ref)
        for i, k in enumerate(ks):
            part = spec[i * chans : (i + 1) * chans]
            spec_ref[k, :, :inner] = part[:, :inner] + gain
            spec_ref[k, :, inner:] = part[:, inner:]


def conv_kernel(
    gated_ref, spec_any, turn_any, fwd_any, bwd_any, out_any, turned_ref, hi_ref, lo_ref, back_ref,
    out_ref, spec_ref, turn_ref, fwd_ref, bwd_ref, sems, out_sems
):
    blocks, inner, chans = gated_ref.shape
    freqs = blocks + 1
    tiles = chans // TILE
    copies = [
        pltpu.make_async_copy(src, dst, sems.at[i])
        for i, (src, dst) in enumerate(
            (
                (turn_any, turn_ref),
                (fwd_any, fwd_ref),
                (bwd_any, bwd_ref),
                (spec_any.at[:, : chans // 2], spec_ref.at[:, : chans // 2]),
                (spec_any.at[:, chans // 2 :], spec_ref.at[:, chans // 2 :]),
            )
        )
    ]
    for copy in copies:
        copy.start()
    for b in range(blocks):
        turned_ref[b] = gated_ref[b].T
    copies[0].wait()

    def outer(t):
        def tile(row):
            xs = [turned_ref[b, t * TILE + row : t * TILE + row + ROWS].astype(F32) for b in range(blocks)]
            for k, (re, im) in enumerate(rfft(xs + [None] * blocks)):
                if k:
                    c, s = turn_ref[0, k : k + 1, :], turn_ref[1, k : k + 1, :]
                    if im is None:
                        re, im = re * c, -(re * s)
                    else:
                        re, im = re * c + im * s, im * c - re * s
                if im is None:
                    im = jnp.zeros_like(re)
                for part, base in ((re, 0), (im, inner)):
                    upper, lower = hi_lo(part)
                    hi_ref[t % 2, k, row : row + ROWS, base : base + inner] = upper
                    lo_ref[t % 2, k, row : row + ROWS, base : base + inner] = lower

        for row in range(0, TILE, ROWS):
            tile(row)

    def flat(x):
        return x.reshape(freqs * TILE, 2 * inner)

    def inverse(t):
        for row in range(0, TILE, ROWS):
            zs = []
            for k in range(freqs):
                re = back_ref[t % 2, k, row : row + ROWS, :inner]
                if k == 0:
                    zs.append((re, None))
                    continue
                im = back_ref[t % 2, k, row : row + ROWS, inner:]
                c, s = turn_ref[0, k : k + 1, :], turn_ref[1, k : k + 1, :]
                zs.append((re * c - im * s, None if k == blocks else re * s + im * c))
            for b, value in enumerate(irfft_first_half(zs)):
                out_ref[b, t * TILE + row : t * TILE + row + ROWS, :] = value.astype(BF16)
        part, last = t // group, (t + 1) % group == 0
        if last:
            here = pl.ds(part * group * TILE, group * TILE)
            sent.append(
                pltpu.make_async_copy(out_ref.at[:, here], out_any.at[:, here], out_sems.at[part])
            )
            sent[-1].start()

    sent, group = [], tiles // out_sems.shape[0]
    outer(0)
    copies[1].wait()
    copies[2].wait()
    for t in range(tiles):
        if t in (0, tiles // 2):
            copies[3 if t == 0 else 4].wait()
        sig = inner_product(flat(hi_ref[t % 2]), flat(lo_ref[t % 2]), fwd_ref)
        if t + 1 < tiles:
            outer(t + 1)
        ker = flat(spec_ref[:, t * TILE : (t + 1) * TILE])
        sig_re, sig_im, ker_re, ker_im = (
            x[:, at : at + inner] for x in (sig, ker) for at in (0, inner)
        )
        prod = jnp.concatenate(
            [sig_re * ker_re - sig_im * ker_im, sig_re * ker_im + sig_im * ker_re], axis=1
        )
        back = inner_product(*hi_lo(prod), bwd_ref)
        back_ref[t % 2] = back.reshape(freqs, TILE, 2 * inner)
        if t:
            inverse(t - 1)
    inverse(tiles - 1)
    for copy in sent:
        copy.wait()


def cost(flops, size):
    return pl.CostEstimate(flops=flops, bytes_accessed=size, transcendentals=0)


def whole(shape):
    return pl.BlockSpec(shape, lambda i: (0,) * len(shape))


def filter_spectrum(filt, gain, tables, blocks):
    forward, _, turns = tables
    chans, inner = filt.shape[0], filt.shape[1] // blocks
    shape = (blocks + 1, chans, 2 * inner)
    return pl.pallas_call(
        spectrum_kernel,
        out_shape=jax.ShapeDtypeStruct(shape, F32),
        scratch_shapes=[pltpu.VMEM(shape, BF16)] * 2,
        compiler_params=pltpu.CompilerParams(vmem_limit_bytes=20 << 20),
        cost_estimate=cost(3 * 10**9, 4 << 20),
        name="filter_spectrum",
    )(filt, gain, turns, forward)


def long_conv(gated, spectrum, tables):
    forward, backward, turns = tables
    blocks, inner, chans = gated.shape
    tile = (2, blocks + 1, TILE, 2 * inner)
    operands = [in_hbm(x) for x in (spectrum, turns, forward, backward)]
    vmem, hbm = (pl.BlockSpec(memory_space=m) for m in (pltpu.VMEM, pl.ANY))
    return pl.pallas_call(
        conv_kernel,
        in_specs=[vmem] + [hbm] * 4,
        out_specs=hbm,
        out_shape=jax.ShapeDtypeStruct((blocks, chans, inner), BF16),
        scratch_shapes=[
            pltpu.VMEM((blocks, chans, inner), BF16),
            pltpu.VMEM(tile, BF16),
            pltpu.VMEM(tile, BF16),
            pltpu.VMEM(tile, F32),
            pltpu.VMEM((blocks, chans, inner), BF16),
        ]
        + [pltpu.VMEM(x.shape, x.dtype) for x in operands]
        + [pltpu.SemaphoreType.DMA((5,)), pltpu.SemaphoreType.DMA((chans // TILE,))],
        compiler_params=pltpu.CompilerParams(vmem_limit_bytes=24 << 20),
        cost_estimate=cost(6 * 10**9, 4 << 20),
        name="long_conv",
    )(gated, *operands)


PAD = 8


def short_sum(pad_ref, taps_ref, lane, rows):
    total = None
    for k in range(taps_ref.shape[0]):
        term = taps_ref[k : k + 1, pl.ds(lane, LANES)] * pad_ref[pl.ds(PAD - k, rows), :]
        total = term if total is None else total + term
    return total


def in_hbm(x):
    return pltpu.with_memory_space_constraint(x, pltpu.HBM)


PIECES = 2


def tail_kernel(stream_ref, out_ref):
    for lane in range(0, stream_ref.shape[0], LANES):
        out_ref[:, pl.ds(lane, LANES)] = stream_ref[pl.ds(lane, LANES), :].T[-PAD:]


def take_kernel(sig_any, key_any, taps_any, rim_ref, held_ref, wide_ref, taps_ref, sems, tap_sem):
    size = held_ref.shape[1] // PIECES
    copies = [
        [
            pltpu.make_async_copy(
                src.at[pl.ds(p * size, size), :],
                held_ref.at[i, pl.ds(p * size, size), :],
                sems.at[i, p],
            )
            for p in range(PIECES)
        ]
        for i, src in enumerate((sig_any, key_any))
    ]
    tap_copy = pltpu.make_async_copy(taps_any, taps_ref, tap_sem)
    for stream in copies:
        for copy in stream:
            copy.start()
    tap_copy.start()
    for i, stream in enumerate(copies):
        for p, copy in enumerate(stream):
            copy.wait()
            for lane in range(p * size, (p + 1) * size, LANES):
                turned = held_ref[i, pl.ds(lane, LANES), :].T
                rim_ref[pl.ds(i * PAD, PAD), pl.ds(lane, LANES)] = turned[-PAD:]
    tap_copy.wait()
    wide_ref[...] = taps_ref[...].astype(F32)


def send_off(part, size, src_ref, dst_any, sems):
    copy = pltpu.make_async_copy(
        src_ref.at[part * size : (part + 1) * size],
        dst_any.at[part * size : (part + 1) * size],
        sems.at[part],
    )
    copy.start()
    return copy


def gate_kernel(held_ref, taps_ref, out_any, head_ref, pad_ref, block_ref, sems):
    blocks, rows, chans = block_ref.shape
    size = blocks // sems.shape[0]
    pad_ref[:, :PAD] = jnp.zeros((2, PAD, LANES), F32)
    copies = []
    for part in range(sems.shape[0]):
        for lane in range(part * size * chans, (part + 1) * size * chans, LANES):
            feats = []
            for i in range(2):
                turned = held_ref[i, pl.ds(lane, LANES), :].T.astype(F32)
                pad_ref[i, pl.ds(PAD, rows), :] = turned
                head_ref[i, :, pl.ds(lane, LANES)] = turned[:ROWS]
                feats.append(short_sum(pad_ref.at[i], taps_ref.at[i], lane, rows))
            block_ref[lane // chans, :, pl.ds(lane % chans, LANES)] = (
                feats[1] * feats[0]
            ).astype(BF16)
        copies.append(send_off(part, size, block_ref, out_any, sems))
    for copy in copies:
        copy.wait()


def rim_kernel(
    head_ref, rim_ref, taps_ref, whole_any, out_any, pad_ref, block_ref, sem
):
    blocks, rows, chans = block_ref.shape
    size = blocks // sem.shape[0]
    copies = []
    for lane in range(0, blocks * chans, LANES):
        feats = []
        for i in range(2):
            pad_ref[i, :PAD] = rim_ref[pl.ds(i * PAD, PAD), pl.ds(lane, LANES)].astype(F32)
            pad_ref[i, PAD:] = head_ref[i, :, pl.ds(lane, LANES)]
            feats.append(short_sum(pad_ref.at[i], taps_ref.at[i], lane, rows))
        block_ref[lane // chans, :, pl.ds(lane % chans, LANES)] = (feats[1] * feats[0]).astype(BF16)
        if (lane + LANES) % (size * chans) == 0:
            part = lane // (size * chans)
            here = pl.ds(part * size, size)
            copies.append(
                pltpu.make_async_copy(block_ref.at[here], out_any.at[here, :rows], sem.at[part])
            )
            copies[-1].start()
    for copy in copies:
        copy.wait()


def query_kernel(query_ref, rim_ref, taps_ref, out_ref, pad_ref):
    rows = query_ref.shape[1]
    for lane in range(0, query_ref.shape[0], LANES):
        pad_ref[:PAD] = rim_ref[:, pl.ds(lane, LANES)].astype(F32)
        pad_ref[PAD:] = query_ref[pl.ds(lane, LANES), :].T.astype(F32)
        out_ref[pl.ds(lane, LANES), :] = short_sum(pad_ref, taps_ref.at[2], lane, rows).T


def mix_kernel(conv_ref, query_ref, out_any, block_ref, sems):
    size = block_ref.shape[0] // sems.shape[0]
    copies = []
    for part in range(sems.shape[0]):
        for b in range(part * size, (part + 1) * size):
            block_ref[b] = (conv_ref[b].astype(F32) * query_ref[b]).astype(BF16)
        copies.append(send_off(part, size, block_ref, out_any, sems))
    for copy in copies:
        copy.wait()


def fast_path(signal, input_gate, output_gate, short_taps, long_filter, bypass_gain):
    channels, rows = signal.shape
    tap_count = short_taps.shape[2]
    chans, length = long_filter.shape
    blocks = length // rows
    taps = short_taps.transpose(0, 2, 1)
    params = pltpu.CompilerParams(vmem_limit_bytes=VMEM_LIMIT)
    some = blocks // 4

    def stream_spec(count):
        return pl.BlockSpec((count * chans, rows), lambda i: (i, 0))

    def block_spec(count):
        return pl.BlockSpec((count, rows, chans), lambda i: (i, 0, 0))

    def taps_spec(count):
        return pl.BlockSpec((3, tap_count, count * chans), lambda i: (0, 0, i))

    vmem, hbm = (pl.BlockSpec(memory_space=m) for m in (pltpu.VMEM, pl.ANY))
    last, held, wide = pl.pallas_call(
        take_kernel,
        in_specs=[hbm] * 3,
        out_specs=[vmem] * 3,
        out_shape=[
            jax.ShapeDtypeStruct((2 * PAD, channels), BF16),
            jax.ShapeDtypeStruct((2, channels, rows), BF16),
            jax.ShapeDtypeStruct(taps.shape, F32),
        ],
        scratch_shapes=[
            pltpu.VMEM(taps.shape, BF16),
            pltpu.SemaphoreType.DMA((2, PIECES)),
            pltpu.SemaphoreType.DMA,
        ],
        compiler_params=params,
        cost_estimate=cost(10**8, 4 << 20),
        name="take",
    )(*(in_hbm(x) for x in (signal, input_gate, taps)))
    rim = shifted(last, "ctx", 1)
    parts = blocks // 2
    gated, head = pl.pallas_call(
        gate_kernel,
        in_specs=[vmem] * 2,
        out_specs=[hbm, vmem],
        out_shape=[
            jax.ShapeDtypeStruct((blocks, rows, chans), BF16),
            jax.ShapeDtypeStruct((2, ROWS, channels), F32),
        ],
        scratch_shapes=[
            pltpu.VMEM((2, PAD + rows, LANES), F32),
            pltpu.VMEM((blocks, rows, chans), BF16),
            pltpu.SemaphoreType.DMA((parts,)),
        ],
        compiler_params=params,
        cost_estimate=cost(10**9, 8 << 20),
        name="gate_main",
    )(held, wide)
    gated = pl.pallas_call(
        rim_kernel,
        in_specs=[vmem] * 3 + [hbm],
        out_specs=hbm,
        out_shape=jax.ShapeDtypeStruct((blocks, rows, chans), BF16),
        scratch_shapes=[
            pltpu.VMEM((2, PAD + ROWS, LANES), F32),
            pltpu.VMEM((blocks, ROWS, chans), BF16),
            pltpu.SemaphoreType.DMA((4,)),
        ],
        input_output_aliases={3: 0},
        compiler_params=params,
        cost_estimate=cost(10**7, 1 << 20),
        name="gate_rim",
    )(head, rim, wide, gated)
    arrived = lax.all_to_all(gated, "ctx", 0, 0)

    tables = transform_tables(blocks, rows)
    gain = bypass_gain.reshape(chans, 1)
    spectrum = filter_spectrum(long_filter, gain, tables, blocks)
    query_last = pl.pallas_call(
        tail_kernel,
        out_shape=jax.ShapeDtypeStruct((PAD, channels), BF16),
        compiler_params=params,
        cost_estimate=cost(10**8, 2 << 20),
        name="query_last",
    )(output_gate)
    query_rim = shifted(query_last, "ctx", 1)
    arrived, query_rim = lax.optimization_barrier((arrived, query_rim))
    query = pl.pallas_call(
        query_kernel,
        grid=(blocks // some,),
        in_specs=[
            stream_spec(some),
            pl.BlockSpec((PAD, some * chans), lambda i: (0, i)),
            taps_spec(some),
        ],
        out_specs=stream_spec(some),
        out_shape=jax.ShapeDtypeStruct((channels, rows), F32),
        scratch_shapes=[pltpu.VMEM((PAD + rows, LANES), F32)],
        compiler_params=params,
        cost_estimate=cost(10**9, 8 << 20),
        name="query_feat",
    )(output_gate, query_rim, wide)

    query = query.reshape(blocks, chans, rows)
    returned = lax.all_to_all(long_conv(arrived, spectrum, tables), "ctx", 0, 0)
    mixed = pl.pallas_call(
        mix_kernel,
        in_specs=[vmem] * 2,
        out_specs=hbm,
        out_shape=jax.ShapeDtypeStruct((blocks, chans, rows), BF16),
        scratch_shapes=[
            pltpu.VMEM((blocks, chans, rows), BF16),
            pltpu.SemaphoreType.DMA((parts,)),
        ],
        compiler_params=params,
        cost_estimate=cost(10**8, 4 << 20),
        name="mix",
    )(returned, query)
    return mixed.reshape(channels, rows)


def on_device(signal, input_gate, output_gate, short_taps, long_filter, bypass_gain):
    channels, rows = signal.shape
    chans, length = long_filter.shape
    blocks = length // rows
    fits = (
        rows == LANES
        and chans % LANES == 0
        and chans * blocks == channels
        and blocks * rows == length
        and blocks in (4, 8, 16)
        and short_taps.shape[2] <= PAD
    )
    path = fast_path if fits else general_path
    return path(signal, input_gate, output_gate, short_taps, long_filter, bypass_gain)


def solution(mesh):
    placed = (
        P(None, ("groups", "ctx")),
        P(None, ("groups", "ctx")),
        P(None, ("groups", "ctx")),
        P(),
        P("ctx", None),
        P("ctx"),
    )
    return jax.shard_map(
        on_device, mesh=mesh, in_specs=placed, out_specs=P(None, ("groups", "ctx")), check_vma=False
    )
```
